256 devices in a mesh: ax: 64 (over z, x, core), rad: 4 (over y).
Axes of the slice: x: 4, y: 4, z: 8, core: 2. Of those that a mesh axis runs over, the one named last changes fastest.
Arguments:
- labels: int32 [8192, 512], P('ax', 'rad'), may hold values from 0 to 2, as said below
- jitter: float32 [8192, 512], P('ax', 'rad'), may hold values from 0.8 to 1.6
Outputs:
- window_state: float32 [6, 8192, 512], P(None, 'ax', 'rad')
- time_steps: float32 [3], replicated
The draws below stay inside these ranges and needn't reach their ends.
Inputs may be any that keep to these rules, and one draw needn't show every extreme that they name: `labels`: 0 unshocked liquid, 1 shocked liquid, 2 gas bubble.
All inputs are finite; a program needn't handle non-finite values.
Results may differ from the reference program's by a relative error of at most 0.0003.
Values sent between devices are 32-bit elements; how exact they have to be, the bound alone decides.
A program may use at most 64 MiB of HBM per device.

```python
import jax
import jax.numpy as jnp
from jax import lax

CX = 128
WIN = 128
STEPS = 3
NX = 8192
NR = 512
N_AX = 64


def draw_labels(key, part):
    subkeys = jax.random.split(jax.random.fold_in(key, 17), 5)
    bubble_radius = max(NR // 10, 2)
    spacing_x = jax.random.randint(subkeys[0], (), 3 * bubble_radius, 5 * bubble_radius + 1)
    spacing_r = jax.random.randint(subkeys[1], (), 3 * bubble_radius, 4 * bubble_radius + 1)
    offset_x = jax.random.randint(subkeys[2], (), 0, 3 * bubble_radius)
    front_column = jax.random.randint(subkeys[3], (), NX // 8, NX // 4 + 1)
    radius_table = jax.random.randint(subkeys[4], (NX,), bubble_radius // 2 + 1, bubble_radius + 1)
    column_ids = jnp.arange(NX, dtype=jnp.int32)[:, None]
    row_ids = jnp.arange(NR, dtype=jnp.int32)[None, :]
    shifted_columns = column_ids + offset_x
    bubble_index = shifted_columns // spacing_x
    axial_gap = shifted_columns - bubble_index * spacing_x - spacing_x // 2
    cycle_index = (row_ids + spacing_r // 2) // spacing_r
    radial_gap = row_ids - cycle_index * spacing_r
    own_radius = radius_table[(bubble_index + 7 * cycle_index) % NX]
    inside = axial_gap * axial_gap + radial_gap * radial_gap < own_radius * own_radius
    shocked = column_ids < front_column
    return jnp.where(inside, 2, jnp.where(shocked, 1, 0)).astype(jnp.int32)


def draw_jitter(key, part):
    subkeys = jax.random.split(jax.random.fold_in(key, 29), 4)
    floor_low = 0.8
    floor_high = 0.9
    global_floor = jax.random.uniform(subkeys[0], (), jnp.float32, floor_low, floor_high)
    block_count = 16
    block_factor = jnp.exp(jax.random.uniform(subkeys[1], (block_count,), jnp.float32, 0.0, 1.0) * jnp.log(1.5))
    lowest_block = jax.random.randint(subkeys[2], (), 0, 2)
    block_ids = jnp.arange(block_count, dtype=jnp.int32)
    block_factor = jnp.where(block_ids == lowest_block, 1.0, block_factor)
    column_ids = jnp.arange(NX, dtype=jnp.int32)
    column_block = column_ids * block_count // NX
    column_onehot = (column_block[:, None] == block_ids[None, :]).astype(jnp.float32)
    column_floor = global_floor * jnp.sum(column_onehot * block_factor[None, :], axis=1)[:, None]
    spread = jax.random.uniform(subkeys[3], (NX, NR), jnp.float32, 0.0, 1.0)
    values = column_floor * jnp.exp(spread * jnp.log(1.6 / column_floor))
    return jnp.clip(values, 0.8, 1.6).astype(jnp.float32)


def setup_inputs(seed: int = 0) -> dict:
    streams_of = jax.random.split(jax.random.key(seed), 3)
    labels = draw_labels(jax.random.fold_in(streams_of[2], 71), 0)
    jitter = draw_jitter(jax.random.fold_in(streams_of[2], 71), 0)
    return {"labels": labels, "jitter": jitter}


G_LIQUID = 4.4
PI_LIQUID = 1.0
G_GAS = 1.4
PI_GAS = 0.0
CFL_NUMBER = 0.3
WENO_EPS = 1e-06
ALPHA_TABLE = (0.99, 0.99, 0.01)
LIQUID_TABLE = (1.0, 1.25, 1.0)
GAS_TABLE = (0.1, 0.1, 0.1)
VELOCITY_TABLE = (0.0, 0.4, 0.0)
PRESSURE_TABLE = (1.0, 3.0, 1.0)
FLIP = (1.0, 1.0, 1.0, -1.0, 1.0, 1.0)

def mixture(fraction):
    gamma_sum = fraction / (G_LIQUID - 1.0) + (1.0 - fraction) / (G_GAS - 1.0)
    stiff_sum = fraction * (G_LIQUID * PI_LIQUID / (G_LIQUID - 1.0)) + (1.0 - fraction) * (G_GAS * PI_GAS / (G_GAS - 1.0))
    return (gamma_sum, stiff_sum)

def initial_fields(labels, jitter):
    phase_ids = jnp.arange(3, dtype=jnp.int32)
    onehot = (labels[None] == phase_ids[:, None, None]).astype(jnp.float32)

    def lookup(table_values):
        return lax.optimization_barrier(jnp.sum(jnp.array(table_values, jnp.float32)[:, None, None] * onehot, axis=0))
    fraction = lookup(ALPHA_TABLE)
    part_one = fraction * lookup(LIQUID_TABLE) * jitter
    part_two = (1.0 - fraction) * lookup(GAS_TABLE) * jitter
    density = part_one + part_two
    velocity = lookup(VELOCITY_TABLE)
    pressure = lookup(PRESSURE_TABLE) * jitter
    gamma_sum, stiff_sum = mixture(fraction)
    energy = gamma_sum * pressure + stiff_sum + 0.5 * density * velocity * velocity
    return jnp.stack([part_one, part_two, density * velocity, jnp.zeros_like(density), energy, fraction])

def primitives(fields):
    density = fields[0] + fields[1]
    axial_speed = fields[2] / density
    radial_speed = fields[3] / density
    gamma_sum, stiff_sum = mixture(fields[5])
    pressure = (fields[4] - 0.5 * density * (axial_speed * axial_speed + radial_speed * radial_speed) - stiff_sum) / gamma_sum
    return jnp.stack([fields[0], fields[1], axial_speed, radial_speed, pressure, fields[5]])

def speed_bound(fields):
    primitive = primitives(fields)
    density = primitive[0] + primitive[1]
    gamma_sum, stiff_sum = mixture(primitive[5])
    celerity = jnp.sqrt(((gamma_sum + 1.0) * primitive[4] + stiff_sum) / (gamma_sum * density))
    return jnp.abs(primitive[2]) + jnp.abs(primitive[3]) + celerity

def weno_side(minus_two, minus_one, middle, plus_one, plus_two):
    cand_zero = (2.0 * minus_two - 7.0 * minus_one + 11.0 * middle) / 6.0
    cand_one = (-minus_one + 5.0 * middle + 2.0 * plus_one) / 6.0
    cand_two = (2.0 * middle + 5.0 * plus_one - plus_two) / 6.0
    smooth_zero = 13.0 / 12.0 * (minus_two - 2.0 * minus_one + middle) ** 2 + 0.25 * (minus_two - 4.0 * minus_one + 3.0 * middle) ** 2
    smooth_one = 13.0 / 12.0 * (minus_one - 2.0 * middle + plus_one) ** 2 + 0.25 * (minus_one - plus_one) ** 2
    smooth_two = 13.0 / 12.0 * (middle - 2.0 * plus_one + plus_two) ** 2 + 0.25 * (3.0 * middle - 4.0 * plus_one + plus_two) ** 2
    weight_zero = 0.1 / (WENO_EPS + smooth_zero) ** 2
    weight_one = 0.6 / (WENO_EPS + smooth_one) ** 2
    weight_two = 0.3 / (WENO_EPS + smooth_two) ** 2
    return (weight_zero * cand_zero + weight_one * cand_one + weight_two * cand_two) / (weight_zero + weight_one + weight_two)

def interfaces(primitive, along_axis):
    span_count = primitive.shape[along_axis] - 5
    stencil = [lax.slice_in_dim(primitive, offset, offset + span_count, axis=along_axis) for offset in range(6)]
    left_state = weno_side(stencil[0], stencil[1], stencil[2], stencil[3], stencil[4])
    right_state = weno_side(stencil[5], stencil[4], stencil[3], stencil[2], stencil[1])
    return (left_state, right_state)

def hllc_flux(left_state, right_state, normal):
    tangent = 5 - normal

    def side_terms(primitive):
        density = primitive[0] + primitive[1]
        gamma_sum, stiff_sum = mixture(primitive[5])
        normal_speed = primitive[normal]
        tangent_speed = primitive[tangent]
        pressure = primitive[4]
        energy = gamma_sum * pressure + stiff_sum + 0.5 * density * (normal_speed * normal_speed + tangent_speed * tangent_speed)
        celerity = jnp.sqrt(((gamma_sum + 1.0) * pressure + stiff_sum) / (gamma_sum * density))
        return (density, normal_speed, tangent_speed, pressure, energy, celerity)
    left_values = side_terms(left_state)
    right_values = side_terms(right_state)
    speed_low = jnp.minimum(left_values[1] - left_values[5], right_values[1] - right_values[5])
    speed_high = jnp.maximum(left_values[1] + left_values[5], right_values[1] + right_values[5])
    left_mass = left_values[0] * (speed_low - left_values[1])
    right_mass = right_values[0] * (speed_high - right_values[1])
    star_speed = (right_values[3] - left_values[3] + left_mass * left_values[1] - right_mass * right_values[1]) / (left_mass - right_mass)

    def arrange(first_part, second_part, normal_part, tangent_part, energy_part):
        components = [first_part, second_part, None, None, energy_part]
        components[normal] = normal_part
        components[tangent] = tangent_part
        return components

    def physical(primitive, side_values):
        density, normal_speed, tangent_speed, pressure, energy, celerity = side_values
        return arrange(primitive[0] * normal_speed, primitive[1] * normal_speed, density * normal_speed * normal_speed + pressure, density * normal_speed * tangent_speed, (energy + pressure) * normal_speed)

    def conserved(primitive, side_values):
        density, normal_speed, tangent_speed, pressure, energy, celerity = side_values
        return arrange(primitive[0], primitive[1], density * normal_speed, density * tangent_speed, energy)

    def starred(primitive, side_values, wave_speed):
        density, normal_speed, tangent_speed, pressure, energy, celerity = side_values
        factor = (wave_speed - normal_speed) / (wave_speed - star_speed)
        star_energy = energy + (star_speed - normal_speed) * (density * star_speed + pressure / (wave_speed - normal_speed))
        return arrange(factor * primitive[0], factor * primitive[1], factor * density * star_speed, factor * density * tangent_speed, factor * star_energy)
    left_flux = physical(left_state, left_values)
    right_flux = physical(right_state, right_values)
    left_cons = conserved(left_state, left_values)
    right_cons = conserved(right_state, right_values)
    left_star = starred(left_state, left_values, speed_low)
    right_star = starred(right_state, right_values, speed_high)
    fluxes = []
    for component in range(5):
        left_star_flux = left_flux[component] + speed_low * (left_star[component] - left_cons[component])
        right_star_flux = right_flux[component] + speed_high * (right_star[component] - right_cons[component])
        fluxes.append(jnp.where(speed_low >= 0.0, left_flux[component], jnp.where(star_speed >= 0.0, left_star_flux, jnp.where(speed_high >= 0.0, right_star_flux, right_flux[component]))))
    fluxes.append(star_speed * jnp.where(star_speed >= 0.0, left_state[5], right_state[5]))
    return (jnp.stack(fluxes), star_speed)

def section_rhs(padded, radius):
    primitive = primitives(padded)
    axial_flux, axial_star = hllc_flux(*interfaces(primitive[:, :, 3:-3], 1), 2)
    radial_flux, radial_star = hllc_flux(*interfaces(primitive[:, 3:-3, :], 2), 3)
    centre = primitive[:, 3:-3, 3:-3]
    energy = padded[4, 3:-3, 3:-3]
    divergence = axial_flux[:, 1:] - axial_flux[:, :-1] + (radial_flux[:, :, 1:] - radial_flux[:, :, :-1])
    stretch = axial_star[1:] - axial_star[:-1] + (radial_star[:, 1:] - radial_star[:, :-1])
    density = centre[0] + centre[1]
    radial_speed = centre[3]
    inverse = radial_speed / radius
    source = [centre[0] * inverse, centre[1] * inverse, density * centre[2] * inverse, density * radial_speed * inverse, (energy + centre[4]) * inverse]
    rates = [-divergence[component] - source[component] for component in range(5)]
    rates.append(-divergence[5] + centre[5] * stretch)
    return jnp.stack(rates)

def fill_edges(padded, margin, axial_first, axial_last, radial_first, radial_last):
    flip_sign = jnp.array(FLIP, jnp.float32)[:, None, None]
    mirror = padded[:, :, margin:2 * margin][:, :, ::-1] * flip_sign
    padded = jnp.where(radial_first, jnp.concatenate([mirror, padded[:, :, margin:]], axis=2), padded)
    top_row = padded[:, :, -margin - 1:-margin]
    padded = jnp.where(radial_last, jnp.concatenate([padded[:, :, :-margin], jnp.repeat(top_row, margin, axis=2)], axis=2), padded)
    low_column = padded[:, margin:margin + 1, :]
    padded = jnp.where(axial_first, jnp.concatenate([jnp.repeat(low_column, margin, axis=1), padded[:, margin:, :]], axis=1), padded)
    high_column = padded[:, -margin - 1:-margin, :]
    padded = jnp.where(axial_last, jnp.concatenate([padded[:, :-margin, :], jnp.repeat(high_column, margin, axis=1)], axis=1), padded)
    return padded

def reference(labels, jitter):
    fields = initial_fields(labels, jitter)
    radius = jnp.arange(NR, dtype=jnp.float32) + 0.5
    block_starts = jnp.arange(N_AX, dtype=jnp.int32) * CX

    def section_rate(current):
        padded = jnp.pad(current, ((0, 0), (3, 3), (3, 3)))
        padded = fill_edges(padded, 3, True, True, True, True)

        def one_block(block_start):
            window_block = lax.dynamic_slice_in_dim(padded, block_start, CX + 6, 1)
            return section_rhs(window_block, radius)
        blocks = lax.map(one_block, block_starts)
        return jnp.transpose(blocks, (1, 0, 2, 3)).reshape(6, NX, NR)
    step_sizes = []
    for step_index in range(STEPS):
        time_step = CFL_NUMBER / jnp.max(speed_bound(fields))
        first_section = fields + time_step * section_rate(fields)
        second_section = 0.75 * fields + 0.25 * (first_section + time_step * section_rate(first_section))
        fields = 1.0 / 3.0 * fields + 2.0 / 3.0 * (second_section + time_step * section_rate(second_section))
        step_sizes.append(time_step)
    ambient = initial_fields(jnp.zeros((1, 1), jnp.int32), jnp.ones((1, 1), jnp.float32))
    inflow = jnp.broadcast_to(ambient, (6, WIN, NR))
    shifted = jnp.concatenate([fields[:, WIN:, :], inflow], axis=1)
    return (shifted, jnp.stack(step_sizes))
```

```python
import functools

import jax
import jax.numpy as jnp
from jax import lax
from jax.experimental import pallas as pl
from jax.experimental.pallas import tpu as pltpu
from jax.sharding import PartitionSpec as P

MESH = pl.DeviceIdType.MESH

STEPS = 3
STAGES = 3 * STEPS
X_CHIPS = 4

G_LIQUID = 4.4
PI_LIQUID = 1.0
G_GAS = 1.4
PI_GAS = 0.0
CFL_NUMBER = 0.3
WENO_EPS = 1e-06
ALPHA_TABLE = (0.99, 0.99, 0.01)
LIQUID_TABLE = (1.0, 1.25, 1.0)
GAS_TABLE = (0.1, 0.1, 0.1)
VELOCITY_TABLE = (0.0, 0.4, 0.0)
PRESSURE_TABLE = (1.0, 3.0, 1.0)

GAMMA_GAS = 1.0 / (G_GAS - 1.0)
GAMMA_SLOPE = 1.0 / (G_LIQUID - 1.0) - GAMMA_GAS
STIFF_GAS = G_GAS * PI_GAS / (G_GAS - 1.0)
STIFF_SLOPE = G_LIQUID * PI_LIQUID / (G_LIQUID - 1.0) - STIFF_GAS

TILES = 16
ROWS = 8
LANES = 128
GHOST = 3
RADIAL_TILES = 1
AXIAL_TILES = 3


def mixture(fraction):
    gamma_sum = GAMMA_GAS + GAMMA_SLOPE * fraction
    stiff_sum = STIFF_SLOPE * fraction
    if STIFF_GAS != 0.0:
        stiff_sum = stiff_sum + STIFF_GAS
    return gamma_sum, stiff_sum


def initial_cells(labels, jitter):
    def lookup(table):
        return jnp.where(labels == 0, table[0], jnp.where(labels == 1, table[1], table[2]))

    fraction = lookup(ALPHA_TABLE)
    part_one = fraction * lookup(LIQUID_TABLE) * jitter
    part_two = (1.0 - fraction) * lookup(GAS_TABLE) * jitter
    speed = lookup(VELOCITY_TABLE)
    pressure = lookup(PRESSURE_TABLE) * jitter
    return part_one, part_two, speed, pressure, fraction


def ambient_cell():
    fraction = ALPHA_TABLE[0]
    part_one = fraction * LIQUID_TABLE[0]
    part_two = (1.0 - fraction) * GAS_TABLE[0]
    density = part_one + part_two
    speed, pressure = VELOCITY_TABLE[0], PRESSURE_TABLE[0]
    gamma_sum, stiff_sum = mixture(fraction)
    energy = gamma_sum * pressure + stiff_sum + 0.5 * density * speed * speed
    return part_one, part_two, density * speed, 0.0, energy, fraction


def celerity_of(density, pressure, gamma_sum, stiff_sum):
    top = gamma_sum * pressure + stiff_sum + pressure
    return top * lax.rsqrt(top * (gamma_sum * density))


def weno_terms(ea, eb, ec, ed, da, db, dc, ta, tb, tc, ga, gb):
    smooth_zero = ta + eb * (eb + da)
    smooth_one = tb + eb * ec
    smooth_two = tc + ec * (ec - dc)
    square_zero = smooth_zero * smooth_zero
    square_one = smooth_one * smooth_one
    square_two = smooth_two * smooth_two
    weight_zero = square_one * square_two
    weight_one = square_zero * square_two
    weight_two = square_zero * square_one
    low = weight_zero * ga
    high = weight_two * gb
    both = low + high
    twice = both + both
    common = 6.0 * weight_one + (weight_zero + weight_two)
    upper = (twice + high) / (common + (weight_two + weight_two))
    lower = (twice + low) / (common + (weight_zero + weight_zero))
    return upper, lower


def weno_cell(cells):
    m2, m1, c, p1, p2 = cells
    ea, eb, ec, ed = m1 - m2, c - m1, p1 - c, p2 - p1
    da, db, dc = eb - ea, ec - eb, ed - ec
    ta, tb, tc = (d * (d * (4.0 / 3.0)) + WENO_EPS for d in (da, db, dc))
    qa, qb, qc = (d * (1.0 / 6.0) for d in (da, db, dc))
    upper, lower = weno_terms(ea, eb, ec, ed, da, db, dc, ta, tb, tc, qb - qa, qc - qb)
    base = c + (qb + qb)
    return base + 0.5 * eb - upper, base - 0.5 * ec + lower


def weno_run(w, count):
    e = w[1:] - w[:-1]
    d = e[1:] - e[:-1]
    t = d * (d * (4.0 / 3.0)) + WENO_EPS
    q = d * (1.0 / 6.0)
    g = q[1:] - q[:-1]
    n = count
    upper, lower = weno_terms(
        e[:n], e[1 : n + 1], e[2 : n + 2], e[3:], d[:n], d[1 : n + 1], d[2:], t[:n], t[1 : n + 1], t[2:], g[:n], g[1:]
    )
    middle = q[1 : n + 1]
    base = w[2 : n + 2] + (middle + middle)
    return base + 0.5 * e[1 : n + 1] - upper, base - 0.5 * e[2 : n + 2] + lower


def hllc(left, right, normal):
    tangent = 5 - normal

    def side(state):
        density = state[0] + state[1]
        gamma_sum, stiff_sum = mixture(state[5])
        inner = gamma_sum * state[4] + stiff_sum
        top = inner + state[4]
        return density, inner, top * lax.rsqrt(top * (gamma_sum * density))

    rho_l, inner_l, c_l = side(left)
    rho_r, inner_r, c_r = side(right)
    n_l, n_r, p_l, p_r = left[normal], right[normal], left[4], right[4]
    low = jnp.minimum(n_l - c_l, n_r - c_r)
    high = jnp.maximum(n_l + c_l, n_r + c_r)
    mass_l = rho_l * (low - n_l)
    mass_r = rho_r * (high - n_r)
    star = (p_r - p_l + mass_l * n_l - mass_r * n_r) / (mass_l - mass_r)
    forward = star >= 0.0
    outer_left = low >= 0.0
    pick = jnp.logical_or(outer_left, forward)

    def chosen(a, b):
        return jnp.where(pick, a, b)

    q_one, q_two = chosen(left[0], right[0]), chosen(left[1], right[1])
    n, t, p = chosen(n_l, n_r), chosen(left[tangent], right[tangent]), chosen(p_l, p_r)
    wave, mass, inner = chosen(low, high), chosen(mass_l, mass_r), chosen(inner_l, inner_r)
    rho = q_one + q_two
    energy = inner + 0.5 * rho * (n * n + t * t)
    plain = jnp.logical_or(outer_left, jnp.logical_and(jnp.logical_not(pick), high < 0.0))
    inverse = 1.0 / (wave - star)
    factor = (wave - n) * inverse
    jump = star - n
    star_energy = factor * energy + jump * (rho * factor * star + p * inverse)
    star_pressure = p + mass * jump
    speed = jnp.where(plain, n, star)
    scaled = jnp.where(plain, n, factor * star)
    energy = jnp.where(plain, energy, star_energy)
    p = jnp.where(plain, p, star_pressure)
    carried = rho * scaled
    along = carried * speed + p
    across = carried * t
    moments = (along, across) if normal == 2 else (across, along)
    fraction = star * jnp.where(forward, left[5], right[5])
    return [q_one * scaled, q_two * scaled, *moments, (energy + p) * speed, fraction, star]


def kernel(
    sizes,
    labels_hbm,
    jitter_hbm,
    out_ref,
    steps_ref,
    own_labels,
    own_jitter,
    labels,
    jitter,
    cells,
    fields,
    base,
    rate,
    upper,
    lower,
    packed,
    turned,
    strip,
    strip_rate,
    edge,
    dt_ref,
    send_axial,
    send_radial,
    recv_axial,
    recv_radial,
    max_first,
    max_second,
    got_first,
    got_second,
    local_sem,
    shift_send,
    shift_recv,
    halo_send,
    halo_recv,
    first_send,
    first_recv,
    second_send,
    second_recv,
):
    z_size, x_size, core_size, rad_size = sizes
    ax_size = z_size * x_size * core_size
    ax, rad = lax.axis_index("ax"), lax.axis_index("rad")
    core = lax.rem(ax, core_size)
    x = lax.rem(lax.div(ax, core_size), x_size)
    z = lax.div(ax, core_size * x_size)

    def at(z, x, core, rad):
        return ((z * x_size + x) * core_size + core, rad)

    first_group = [
        at(lax.rem(z + dz, z_size), x, lax.rem(core + dc, core_size), rad)
        for dz in range(z_size)
        for dc in range(core_size)
        if (dz, dc) != (0, 0)
    ]
    second_group = [
        at(z, lax.rem(x + dx, x_size), core, lax.rem(rad + dr, rad_size))
        for dx in range(x_size)
        for dr in range(rad_size)
        if (dx, dr) != (0, 0)
    ]
    ax_next = (lax.rem(ax + 1, ax_size), rad)
    ax_last = (lax.rem(ax + ax_size - 1, ax_size), rad)
    rad_next = (ax, lax.rem(rad + 1, rad_size))
    rad_last = (ax, lax.rem(rad + rad_size - 1, rad_size))

    block_first = ax == ax_size - 1
    block_last = ax == ax_size - 2
    wall = rad == 0
    outer = rad == rad_size - 1

    lane = lax.broadcasted_iota(jnp.int32, (ROWS, LANES), 1)
    row = lax.broadcasted_iota(jnp.int32, (ROWS, LANES), 0)

    copies = [
        pltpu.make_async_copy(labels_hbm, own_labels, local_sem.at[0]),
        pltpu.make_async_copy(jitter_hbm, own_jitter, local_sem.at[1]),
    ]
    for copy in copies:
        copy.start()
    barrier = pltpu.get_barrier_semaphore()
    greeted = first_group + second_group + [ax_next, ax_last]
    for device in greeted:
        pl.semaphore_signal(barrier, inc=1, device_id=device, device_id_type=MESH)
    for copy in copies:
        copy.wait()

    def first_copies(step):
        return [
            pltpu.make_async_remote_copy(
                src_ref=max_first.at[step],
                dst_ref=got_first.at[step, i],
                send_sem=first_send.at[step, i],
                recv_sem=first_recv.at[step, i],
                device_id=device,
                device_id_type=MESH,
            )
            for i, device in enumerate(first_group)
        ]

    def second_copies(step):
        return [
            pltpu.make_async_remote_copy(
                src_ref=max_second.at[step],
                dst_ref=got_second.at[step, i],
                send_sem=second_send.at[step, i],
                recv_sem=second_recv.at[step, i],
                device_id=device,
                device_id_type=MESH,
            )
            for i, device in enumerate(second_group)
        ]

    def halo_copies(stage):
        pairs = [
            (send_axial.at[1], recv_axial.at[stage, 0], ax_next),
            (send_axial.at[0], recv_axial.at[stage, 1], ax_last),
            (send_radial.at[1], recv_radial.at[stage, 0], rad_next),
            (send_radial.at[0], recv_radial.at[stage, 1], rad_last),
        ]
        return [
            pltpu.make_async_remote_copy(
                src_ref=source,
                dst_ref=target,
                send_sem=halo_send.at[stage, i],
                recv_sem=halo_recv.at[stage, i],
                device_id=device,
                device_id_type=MESH,
            )
            for i, (source, target, device) in enumerate(pairs)
        ]

    def own_speed(t, most):
        part_one, part_two, speed, pressure, fraction = initial_cells(
            own_labels[pl.ds(t * ROWS, ROWS), :], own_jitter[pl.ds(t * ROWS, ROWS), :]
        )
        celerity = celerity_of(part_one + part_two, pressure, *mixture(fraction))
        return jnp.maximum(most, jnp.abs(speed) + celerity)

    most = lax.fori_loop(0, TILES, own_speed, jnp.zeros((ROWS, LANES), jnp.float32))
    max_first[0] = jnp.max(most, axis=0, keepdims=True)

    pl.semaphore_wait(barrier, len(greeted))
    for copy in first_copies(0):
        copy.start()
    shifts = [
        pltpu.make_async_remote_copy(
            src_ref=source,
            dst_ref=target,
            send_sem=shift_send.at[i],
            recv_sem=shift_recv.at[i],
            device_id=ax_last,
            device_id_type=MESH,
        )
        for i, (source, target) in enumerate(((labels_hbm, labels), (jitter_hbm, jitter)))
    ]
    for copy in shifts:
        copy.start()
    for copy in shifts:
        copy.wait()

    def start_cells(t, carry):
        rows = pl.ds(t, ROWS, stride=TILES)
        part_one, part_two, speed, pressure, fraction = initial_cells(labels[rows, :], jitter[rows, :])
        density = part_one + part_two
        gamma_sum, stiff_sum = mixture(fraction)
        still = jnp.zeros_like(density)
        energy = gamma_sum * pressure + stiff_sum + 0.5 * density * speed * speed
        for i, value in enumerate((part_one, part_two, density * speed, still, energy, fraction)):
            fields[i, t] = value
            base[i, t] = value
        for i, value in enumerate((part_one, part_two, speed, still, pressure, fraction)):
            cells[i, GHOST + t] = value
        return carry

    lax.fori_loop(0, TILES, start_cells, 0)

    radius = (rad * LANES + lane).astype(jnp.float32) + 0.5

    def stage_body(stage, carry):
        step = lax.div(stage, 3)
        section = stage - 3 * step
        halos = halo_copies(stage)

        for i in range(6):
            for k in range(GHOST):
                send_axial[0, 3 * i + k] = cells[i, GHOST + k, 0:1, :]
                send_axial[1, 3 * i + k] = cells[i, TILES + k, ROWS - 1 : ROWS, :]
        halos[0].start()
        halos[1].start()

        def pack(t, carry):
            total = pltpu.roll(cells[0, GHOST + t], (0 - 122) % LANES, 1)
            for i in range(1, 6):
                rolled = pltpu.roll(cells[i, GHOST + t], (12 * i - 122) % LANES, 1)
                total = jnp.where(lane >= 12 * i, rolled, total)
            packed[t] = total
            return carry

        lax.fori_loop(0, TILES, pack, 0)
        turned[...] = packed[...].reshape(LANES, LANES).T
        for i in range(6):
            send_radial[1, 3 * i : 3 * i + 3, :] = turned[12 * i + 3 : 12 * i + 6, :]
            send_radial[0, 3 * i : 3 * i + 3, :] = turned[12 * i + 6 : 12 * i + 9, :]
        halos[2].start()
        halos[3].start()
        for i in range(6):
            strip[i, pl.ds(1, 6, stride=2), :] = turned[12 * i : 12 * i + 6, :]
            strip[i, pl.ds(6, 6, stride=2), :] = turned[12 * i + 6 : 12 * i + 12, :]

        def radial(r, carry):
            tiles = pl.ds(GHOST + r * RADIAL_TILES, RADIAL_TILES)
            left, right = [], []
            for i in range(6):
                w = cells[i, tiles]
                around = [pltpu.roll(w, shift, 2) if shift else w for shift in (2, 1, 0, LANES - 1, LANES - 2)]
                up, down = weno_cell(around)
                left.append(pltpu.roll(up, 1, 2))
                right.append(down)
            flux = hllc(left, right, 3)
            change = [value - pltpu.roll(value, LANES - 1, 2) for value in flux]
            change[5] = change[5] - cells[5, tiles] * change[6]
            for i in range(6):
                rate[i, pl.ds(r * RADIAL_TILES, RADIAL_TILES)] = change[i]
            return carry

        lax.fori_loop(0, TILES // RADIAL_TILES, radial, 0)

        @pl.when(section == 0)
        def _():
            sends = first_copies(step)
            for copy in sends:
                copy.wait_recv()
            max_second[step] = jnp.maximum(max_first[step], jnp.max(got_first[step], axis=0))
            for copy in second_copies(step):
                copy.start()

        halos[0].wait_recv()
        halos[1].wait_recv()
        for i in range(6):
            first_row = cells[i, GHOST, 0:1, :]
            last_row = cells[i, GHOST + TILES - 1, ROWS - 1 : ROWS, :]
            for k in range(GHOST):
                before = jnp.where(block_first, first_row, recv_axial[stage, 0, 3 * i + k])
                after = jnp.where(block_last, last_row, recv_axial[stage, 1, 3 * i + k])
                cells[i, k] = jnp.where(row == 0, before, pltpu.roll(cells[i, TILES + k], 1, 0))
                cells[i, GHOST + TILES + k] = jnp.where(
                    row == ROWS - 1, after, pltpu.roll(cells[i, GHOST + k], ROWS - 1, 0)
                )

        def axial_states(i, carry):
            def chunk(r, carry):
                w = cells[i, pl.ds(r * AXIAL_TILES, AXIAL_TILES + 4)]
                up, down = weno_run(w, AXIAL_TILES)
                upper[i, pl.ds(r * AXIAL_TILES, AXIAL_TILES)] = up
                lower[i, pl.ds(r * AXIAL_TILES, AXIAL_TILES)] = down
                return carry

            return lax.fori_loop(0, (TILES + 2) // AXIAL_TILES, chunk, carry)

        lax.fori_loop(0, 6, axial_states, 0)

        halos[2].wait_recv()
        halos[3].wait_recv()
        for i in range(6):
            sign = -1.0 if i == 3 else 1.0
            for k in range(GHOST):
                mirror = strip[i, 2 * (5 - k) : 2 * (5 - k) + 1, :] * sign
                strip[i, 2 * k : 2 * k + 1, :] = jnp.where(
                    wall, mirror, recv_radial[stage, 0, 3 * i + k : 3 * i + k + 1, :]
                )
                nearest = strip[i, 11:12, :]
                strip[i, 2 * k + 13 : 2 * k + 14, :] = jnp.where(
                    outer, nearest, recv_radial[stage, 1, 3 * i + k : 3 * i + k + 1, :]
                )
        left, right = [], []
        for i in range(6):
            w = [strip[i, 2 * k : 2 * k + 8, :] for k in range(6)]
            left.append(weno_cell(w[:5])[0])
            right.append(weno_cell(w[1:])[1])
        flux = hllc(left, right, 3)
        change = [value - pltpu.roll(value, ROWS - 2, 0) for value in flux]
        change[5] = change[5] - strip[5, 6:14, :] * change[6]
        for i in range(6):
            strip_rate[i] = change[i]
        for i in range(6):
            turned[8 * i : 8 * i + 3, :] = strip_rate[i, pl.ds(1, 3, stride=2), :]
            turned[8 * i + 3 : 8 * i + 6, :] = strip_rate[i, pl.ds(0, 3, stride=2), :]
        edge[...] = turned[...].T.reshape(TILES, ROWS, LANES)

        def axial_flux(f):
            return hllc([upper[i, f] for i in range(6)], [lower[i, f + 1] for i in range(6)], 2)

        def axial(t, carry):
            below = carry
            above = axial_flux(t + 1)
            at_edge = jnp.logical_or(lane < GHOST, lane >= LANES - GHOST)
            strips = edge[t]
            q_one, q_two, u, v, p, a = (cells[i, GHOST + t] for i in range(6))
            over = v / radius
            carried = (q_one + q_two) * over
            source = (q_one * over, q_two * over, u * carried, v * carried, (fields[4, t] + p) * over)
            for i in range(6):
                rim = pltpu.roll(strips, (LANES - GHOST - 8 * i) % LANES, 1)
                radial_part = jnp.where(at_edge, rim, rate[i, t])
                axial_part = below[i] - above[i]
                last = -source[i] if i < 5 else a * (above[6] - below[6])
                rate[i, t] = radial_part + axial_part + last
            return tuple(above)

        lax.fori_loop(0, TILES, axial, tuple(axial_flux(0)))

        @pl.when(section == 0)
        def _():
            sends = second_copies(step)
            for copy in sends:
                copy.wait_recv()
            top = jnp.maximum(max_second[step], jnp.max(got_second[step], axis=0))
            dt = CFL_NUMBER / jnp.broadcast_to(jnp.max(top, axis=1, keepdims=True), (ROWS, LANES))
            dt_ref[...] = dt
            steps_ref[step] = jnp.max(dt)
            for copy in sends:
                copy.wait_send()
            for copy in first_copies(step):
                copy.wait_send()

        for copy in halos:
            copy.wait_send()

        third = jnp.float32(1.0 / 3.0)
        keep = jnp.where(section == 0, 0.0, jnp.where(section == 1, 0.75, third))
        take = jnp.where(section == 0, 1.0, jnp.where(section == 1, 0.25, jnp.float32(2.0 / 3.0)))
        closing = section == 2

        def update(t, most):
            dt = dt_ref[...]
            new = []
            for i in range(6):
                value = keep * base[i, t] + take * (fields[i, t] + dt * rate[i, t])
                fields[i, t] = value
                base[i, t] = jnp.where(closing, value, base[i, t])
                new.append(value)
            density = new[0] + new[1]
            gamma_sum, stiff_sum = mixture(new[5])
            inverse = 1.0 / (density * gamma_sum)
            per_density = inverse * gamma_sum
            u = new[2] * per_density
            v = new[3] * per_density
            p = (new[4] - 0.5 * (new[2] * u + new[3] * v) - stiff_sum) * (inverse * density)
            for i, value in enumerate((new[0], new[1], u, v, p, new[5])):
                cells[i, GHOST + t] = value
            speed = jnp.abs(u) + jnp.abs(v) + celerity_of(density, p, gamma_sum, stiff_sum)
            return jnp.maximum(most, speed)

        most = lax.fori_loop(0, TILES, update, jnp.zeros((ROWS, LANES), jnp.float32))

        @pl.when(jnp.logical_and(closing, step < STEPS - 1))
        def _():
            max_first[step + 1] = jnp.max(most, axis=0, keepdims=True)
            for copy in first_copies(step + 1):
                copy.start()

        return carry

    lax.fori_loop(0, STAGES, stage_body, 0)

    def finish(t, carry):
        for i, value in enumerate(ambient_cell()):
            out_ref[i, pl.ds(t, ROWS, stride=TILES), :] = jnp.where(block_first, jnp.float32(value), fields[i, t])
        return carry

    lax.fori_loop(0, TILES, finish, 0)


def solution(mesh):
    ax_size, rad_size = mesh.shape["ax"], mesh.shape["rad"]
    sizes = (ax_size // (2 * X_CHIPS), X_CHIPS, 2, rad_size)
    first = sizes[0] * sizes[2] - 1
    second = sizes[1] * sizes[3] - 1

    def shards(labels, jitter):
        block = labels.shape
        f32 = jnp.float32
        tile = (TILES, ROWS, LANES)
        dma = pltpu.SemaphoreType.DMA
        return pl.pallas_call(
            functools.partial(kernel, sizes),
            out_shape=(jax.ShapeDtypeStruct((6, *block), f32), jax.ShapeDtypeStruct((STEPS,), f32)),
            in_specs=[pl.BlockSpec(memory_space=pl.ANY)] * 2,
            out_specs=(pl.BlockSpec(memory_space=pltpu.VMEM), pl.BlockSpec(memory_space=pltpu.SMEM)),
            scratch_shapes=[
                pltpu.VMEM(block, jnp.int32),
                pltpu.VMEM(block, f32),
                pltpu.VMEM(block, jnp.int32),
                pltpu.VMEM(block, f32),
                pltpu.VMEM((6, TILES + 2 * GHOST, ROWS, LANES), f32),
                pltpu.VMEM((6, *tile), f32),
                pltpu.VMEM((6, *tile), f32),
                pltpu.VMEM((6, *tile), f32),
                pltpu.VMEM((6, TILES + 2, ROWS, LANES), f32),
                pltpu.VMEM((6, TILES + 2, ROWS, LANES), f32),
                pltpu.VMEM(tile, f32),
                pltpu.VMEM((LANES, LANES), f32),
                pltpu.VMEM((6, 24, LANES), f32),
                pltpu.VMEM((6, ROWS, LANES), f32),
                pltpu.VMEM(tile, f32),
                pltpu.VMEM((ROWS, LANES), f32),
                pltpu.VMEM((2, 18, 1, LANES), f32),
                pltpu.VMEM((2, 24, LANES), f32),
                pltpu.VMEM((STAGES, 2, 18, 1, LANES), f32),
                pltpu.VMEM((STAGES, 2, 24, LANES), f32),
                pltpu.VMEM((STEPS, 1, LANES), f32),
                pltpu.VMEM((STEPS, 1, LANES), f32),
                pltpu.VMEM((STEPS, first, 1, LANES), f32),
                pltpu.VMEM((STEPS, second, 1, LANES), f32),
                dma((2,)),
                dma((2,)),
                dma((2,)),
                dma((STAGES, 4)),
                dma((STAGES, 4)),
                dma((STEPS, first)),
                dma((STEPS, first)),
                dma((STEPS, second)),
                dma((STEPS, second)),
            ],
            compiler_params=pltpu.CompilerParams(collective_id=0, has_side_effects=True),
        )(labels, jitter)

    return jax.shard_map(
        shards, mesh=mesh, in_specs=(P("ax", "rad"),) * 2, out_specs=(P(None, "ax", "rad"), P()), check_vma=False
    )
```

```python
import functools

import jax
import jax.numpy as jnp
from jax import lax
from jax.experimental import pallas as pl
from jax.experimental.pallas import tpu as pltpu
from jax.sharding import PartitionSpec as P

MESH = pl.DeviceIdType.MESH

STEPS = 3
STAGES = 3 * STEPS
X_CHIPS = 4

G_LIQUID = 4.4
PI_LIQUID = 1.0
G_GAS = 1.4
PI_GAS = 0.0
CFL_NUMBER = 0.3
WENO_EPS = 1e-06
ALPHA_TABLE = (0.99, 0.99, 0.01)
LIQUID_TABLE = (1.0, 1.25, 1.0)
GAS_TABLE = (0.1, 0.1, 0.1)
VELOCITY_TABLE = (0.0, 0.4, 0.0)
PRESSURE_TABLE = (1.0, 3.0, 1.0)

GAMMA_GAS = 1.0 / (G_GAS - 1.0)
GAMMA_SLOPE = 1.0 / (G_LIQUID - 1.0) - GAMMA_GAS
STIFF_GAS = G_GAS * PI_GAS / (G_GAS - 1.0)
STIFF_SLOPE = G_LIQUID * PI_LIQUID / (G_LIQUID - 1.0) - STIFF_GAS

TILES = 16
ROWS = 8
LANES = 128
GHOST = 3
FACES = 3
UPDATES = 2
INNER = 12


def mixture(fraction):
    gamma_sum = GAMMA_GAS + GAMMA_SLOPE * fraction
    stiff_sum = STIFF_SLOPE * fraction
    if STIFF_GAS != 0.0:
        stiff_sum = stiff_sum + STIFF_GAS
    return gamma_sum, stiff_sum


def initial_cells(labels, jitter):
    def lookup(table):
        return jnp.where(labels == 0, table[0], jnp.where(labels == 1, table[1], table[2]))

    fraction = lookup(ALPHA_TABLE)
    part_one = fraction * lookup(LIQUID_TABLE) * jitter
    part_two = (1.0 - fraction) * lookup(GAS_TABLE) * jitter
    speed = lookup(VELOCITY_TABLE)
    pressure = lookup(PRESSURE_TABLE) * jitter
    return part_one, part_two, speed, pressure, fraction


def ambient_cell():
    fraction = ALPHA_TABLE[0]
    part_one = fraction * LIQUID_TABLE[0]
    part_two = (1.0 - fraction) * GAS_TABLE[0]
    density = part_one + part_two
    speed, pressure = VELOCITY_TABLE[0], PRESSURE_TABLE[0]
    gamma_sum, stiff_sum = mixture(fraction)
    energy = gamma_sum * pressure + stiff_sum + 0.5 * density * speed * speed
    return part_one, part_two, density * speed, 0.0, energy, fraction


def celerity_of(density, pressure, gamma_sum, stiff_sum):
    top = gamma_sum * pressure + stiff_sum + pressure
    return top * lax.rsqrt(top * (gamma_sum * density))


def weno_terms(ea, eb, ec, ed, da, db, dc, ta, tb, tc, ga, gb):
    smooth_zero = ta + eb * (eb + da)
    smooth_one = tb + eb * ec
    smooth_two = tc + ec * (ec - dc)
    square_zero = smooth_zero * smooth_zero
    square_one = smooth_one * smooth_one
    square_two = smooth_two * smooth_two
    weight_zero = square_one * square_two
    weight_one = square_zero * square_two
    weight_two = square_zero * square_one
    low = weight_zero * ga
    high = weight_two * gb
    both = low + high
    twice = both + both
    common = 6.0 * weight_one + (weight_zero + weight_two)
    upper = (twice + high) / (common + (weight_two + weight_two))
    lower = (twice + low) / (common + (weight_zero + weight_zero))
    return upper, lower


def weno_run(w, count):
    e = w[1:] - w[:-1]
    d = e[1:] - e[:-1]
    t = d * (d * (4.0 / 3.0)) + WENO_EPS
    q = d * (1.0 / 6.0)
    g = q[1:] - q[:-1]
    n = count
    upper, lower = weno_terms(
        e[:n], e[1 : n + 1], e[2 : n + 2], e[3:], d[:n], d[1 : n + 1], d[2:], t[:n], t[1 : n + 1], t[2:], g[:n], g[1:]
    )
    middle = q[1 : n + 1]
    base = w[2 : n + 2] + (middle + middle)
    return base + 0.5 * e[1 : n + 1] - upper, base - 0.5 * e[2 : n + 2] + lower


def hllc(left, right, normal):
    tangent = 5 - normal

    def side(state):
        density = state[0] + state[1]
        gamma_sum, stiff_sum = mixture(state[5])
        inner = gamma_sum * state[4] + stiff_sum
        top = inner + state[4]
        return density, inner, top * lax.rsqrt(top * (gamma_sum * density))

    rho_l, inner_l, c_l = side(left)
    rho_r, inner_r, c_r = side(right)
    n_l, n_r, p_l, p_r = left[normal], right[normal], left[4], right[4]
    low = jnp.minimum(n_l - c_l, n_r - c_r)
    high = jnp.maximum(n_l + c_l, n_r + c_r)
    mass_l = rho_l * (low - n_l)
    mass_r = rho_r * (high - n_r)
    star = (p_r - p_l + mass_l * n_l - mass_r * n_r) / (mass_l - mass_r)
    forward = star >= 0.0
    outer_left = low >= 0.0
    pick = jnp.logical_or(outer_left, forward)

    def chosen(a, b):
        return jnp.where(pick, a, b)

    q_one, q_two = chosen(left[0], right[0]), chosen(left[1], right[1])
    n, t, p = chosen(n_l, n_r), chosen(left[tangent], right[tangent]), chosen(p_l, p_r)
    wave, mass, inner = chosen(low, high), chosen(mass_l, mass_r), chosen(inner_l, inner_r)
    rho = q_one + q_two
    energy = inner + 0.5 * rho * (n * n + t * t)
    plain = jnp.logical_or(outer_left, jnp.logical_and(jnp.logical_not(pick), high < 0.0))
    inverse = 1.0 / (wave - star)
    factor = (wave - n) * inverse
    jump = star - n
    star_energy = factor * energy + jump * (rho * factor * star + p * inverse)
    star_pressure = p + mass * jump
    speed = jnp.where(plain, n, star)
    scaled = jnp.where(plain, n, factor * star)
    energy = jnp.where(plain, energy, star_energy)
    p = jnp.where(plain, p, star_pressure)
    carried = rho * scaled
    along = carried * speed + p
    across = carried * t
    moments = (along, across) if normal == 2 else (across, along)
    fraction = star * jnp.where(forward, left[5], right[5])
    return [q_one * scaled, q_two * scaled, *moments, (energy + p) * speed, fraction, star]


def kernel(
    sizes,
    labels_hbm,
    jitter_hbm,
    out_ref,
    steps_ref,
    own_labels,
    own_jitter,
    labels,
    jitter,
    axial_cells,
    radial_cells,
    fields,
    base,
    upper,
    lower,
    axial_rate,
    radial_rate,
    turned,
    dt_ref,
    send_axial,
    send_radial,
    recv_axial,
    recv_radial,
    max_first,
    max_second,
    got_first,
    got_second,
    local_sem,
    shift_send,
    shift_recv,
    halo_send,
    halo_recv,
    first_send,
    first_recv,
    second_send,
    second_recv,
):
    z_size, x_size, core_size, rad_size = sizes
    ax_size = z_size * x_size * core_size
    ax, rad = lax.axis_index("ax"), lax.axis_index("rad")
    core = lax.rem(ax, core_size)
    x = lax.rem(lax.div(ax, core_size), x_size)
    z = lax.div(ax, core_size * x_size)

    def at(z, x, core, rad):
        return ((z * x_size + x) * core_size + core, rad)

    first_group = [
        at(lax.rem(z + dz, z_size), x, lax.rem(core + dc, core_size), rad)
        for dz in range(z_size)
        for dc in range(core_size)
        if (dz, dc) != (0, 0)
    ]
    second_group = [
        at(z, lax.rem(x + dx, x_size), core, lax.rem(rad + dr, rad_size))
        for dx in range(x_size)
        for dr in range(rad_size)
        if (dx, dr) != (0, 0)
    ]
    ax_next = (lax.rem(ax + 1, ax_size), rad)
    ax_last = (lax.rem(ax + ax_size - 1, ax_size), rad)
    rad_next = (ax, lax.rem(rad + 1, rad_size))
    rad_last = (ax, lax.rem(rad + rad_size - 1, rad_size))

    block_first = ax == ax_size - 1
    block_last = ax == ax_size - 2
    wall = rad == 0
    outer = rad == rad_size - 1

    lane = lax.broadcasted_iota(jnp.int32, (ROWS, LANES), 1)
    row = lax.broadcasted_iota(jnp.int32, (ROWS, LANES), 0)

    copies = [
        pltpu.make_async_copy(labels_hbm, own_labels, local_sem.at[0]),
        pltpu.make_async_copy(jitter_hbm, own_jitter, local_sem.at[1]),
    ]
    for copy in copies:
        copy.start()
    barrier = pltpu.get_barrier_semaphore()
    greeted = first_group + second_group + [ax_next, ax_last]
    for device in greeted:
        pl.semaphore_signal(barrier, inc=1, device_id=device, device_id_type=MESH)
    for copy in copies:
        copy.wait()

    def first_copies(step):
        return [
            pltpu.make_async_remote_copy(
                src_ref=max_first.at[step],
                dst_ref=got_first.at[step, i],
                send_sem=first_send.at[step, i],
                recv_sem=first_recv.at[step, i],
                device_id=device,
                device_id_type=MESH,
            )
            for i, device in enumerate(first_group)
        ]

    def second_copies(step):
        return [
            pltpu.make_async_remote_copy(
                src_ref=max_second.at[step],
                dst_ref=got_second.at[step, i],
                send_sem=second_send.at[step, i],
                recv_sem=second_recv.at[step, i],
                device_id=device,
                device_id_type=MESH,
            )
            for i, device in enumerate(second_group)
        ]

    def halo_copies(stage):
        pairs = [
            (send_axial.at[1], recv_axial.at[stage, 0], ax_next),
            (send_axial.at[0], recv_axial.at[stage, 1], ax_last),
            (send_radial.at[1], recv_radial.at[stage, 0], rad_next),
            (send_radial.at[0], recv_radial.at[stage, 1], rad_last),
        ]
        return [
            pltpu.make_async_remote_copy(
                src_ref=source,
                dst_ref=target,
                send_sem=halo_send.at[stage, i],
                recv_sem=halo_recv.at[stage, i],
                device_id=device,
                device_id_type=MESH,
            )
            for i, (source, target, device) in enumerate(pairs)
        ]

    def own_speed(t, most):
        part_one, part_two, speed, pressure, fraction = initial_cells(
            own_labels[pl.ds(t * ROWS, ROWS), :], own_jitter[pl.ds(t * ROWS, ROWS), :]
        )
        celerity = celerity_of(part_one + part_two, pressure, *mixture(fraction))
        return jnp.maximum(most, jnp.abs(speed) + celerity)

    most = lax.fori_loop(0, TILES, own_speed, jnp.zeros((ROWS, LANES), jnp.float32))
    max_first[0] = jnp.max(most, axis=0, keepdims=True)

    pl.semaphore_wait(barrier, len(greeted))
    for copy in first_copies(0):
        copy.start()
    shifts = [
        pltpu.make_async_remote_copy(
            src_ref=source,
            dst_ref=target,
            send_sem=shift_send.at[i],
            recv_sem=shift_recv.at[i],
            device_id=ax_last,
            device_id_type=MESH,
        )
        for i, (source, target) in enumerate(((labels_hbm, labels), (jitter_hbm, jitter)))
    ]
    for copy in shifts:
        copy.start()
    for copy in shifts:
        copy.wait()

    to_lanes = (lane % ROWS) * TILES + lane // ROWS
    from_lanes = (lane % TILES) * ROWS + lane // TILES

    def start_cells(t, carry):
        rows = pl.ds(t, ROWS, stride=TILES)
        part_one, part_two, speed, pressure, fraction = initial_cells(
            jnp.take_along_axis(labels[rows, :], to_lanes, axis=1), jnp.take_along_axis(jitter[rows, :], to_lanes, axis=1)
        )
        density = part_one + part_two
        gamma_sum, stiff_sum = mixture(fraction)
        still = jnp.zeros_like(density)
        energy = gamma_sum * pressure + stiff_sum + 0.5 * density * speed * speed
        for i, value in enumerate((part_one, part_two, density * speed, still, energy, fraction)):
            fields[i, t] = value
            base[i, t] = value
        for i, value in enumerate((part_one, part_two, speed, still, pressure, fraction)):
            axial_cells[i, GHOST + t] = value
        return carry

    lax.fori_loop(0, TILES, start_cells, 0)

    radius = (rad * LANES + to_lanes).astype(jnp.float32) + 0.5
    per_radius = 1.0 / radius

    def take_rims(cells, send):
        for i in range(6):
            for k in range(GHOST):
                send[0, 3 * i + k] = cells[i, GHOST + k, 0:1, :]
                send[1, 3 * i + k] = cells[i, TILES + k, ROWS - 1 : ROWS, :]

    def ghosts(cells, recv, stage, at_low, at_high, mirrored):
        for i in range(6):
            for k in range(GHOST):
                if mirrored:
                    low = cells[i, 2 * GHOST - 1 - k, 0:1, :]
                    if i == 3:
                        low = -low
                else:
                    low = cells[i, GHOST, 0:1, :]
                high = cells[i, GHOST + TILES - 1, ROWS - 1 : ROWS, :]
                before = jnp.where(at_low, low, recv[stage, 0, 3 * i + k])
                after = jnp.where(at_high, high, recv[stage, 1, 3 * i + k])
                cells[i, k] = jnp.where(row == 0, before, pltpu.roll(cells[i, TILES + k], 1, 0))
                cells[i, GHOST + TILES + k] = jnp.where(
                    row == ROWS - 1, after, pltpu.roll(cells[i, GHOST + k], ROWS - 1, 0)
                )

    def states(cells, which, i, first, count):
        up, down = weno_run(cells[i, first : first + count + 4], count)
        upper[which, i, first : first + count] = up
        lower[which, i, first : first + count] = down

    def rim_states(cells, which):
        def one(i, carry):
            states(cells, which, i, 0, 3)
            states(cells, which, i, 15, 3)
            return carry

        lax.fori_loop(0, 6, one, 0)

    def faces(cells, which, rate, normal):
        def some(r, below):
            for k in range(FACES):
                f = r * FACES + k
                above = hllc([upper[which, i, f] for i in range(6)], [lower[which, i, f + 1] for i in range(6)], normal)
                change = [b - a for b, a in zip(below, above)]
                change[5] = change[5] - cells[5, f + 2] * change[6]
                for i in range(6):
                    rate[i, f] = change[i]
                below = tuple(above)
            return below

        lax.fori_loop(0, (TILES + 2) // FACES, some, (jnp.zeros((ROWS, LANES), jnp.float32),) * 7)

    def stage_body(stage, carry):
        step = lax.div(stage, 3)
        section = stage - 3 * step
        halos = halo_copies(stage)

        take_rims(axial_cells, send_axial)
        halos[0].start()
        halos[1].start()

        def turn(i, carry):
            block = axial_cells[i, GHOST : GHOST + TILES].reshape(LANES, LANES)
            radial_cells[i, GHOST : GHOST + TILES] = block.T.reshape(TILES, ROWS, LANES)
            for first in range(3, 15, INNER):
                states(axial_cells, 0, i, first, INNER)
            return carry

        lax.fori_loop(0, 6, turn, 0)
        take_rims(radial_cells, send_radial)
        halos[2].start()
        halos[3].start()

        def inner(i, carry):
            for first in range(3, 15, INNER):
                states(radial_cells, 1, i, first, INNER)
            return carry

        lax.fori_loop(0, 6, inner, 0)

        halos[0].wait_recv()
        halos[1].wait_recv()
        ghosts(axial_cells, recv_axial, stage, block_first, block_last, False)
        rim_states(axial_cells, 0)
        faces(axial_cells, 0, axial_rate, 2)

        @pl.when(section == 0)
        def _():
            sends = first_copies(step)
            for copy in sends:
                copy.wait_recv()
            max_second[step] = jnp.maximum(max_first[step], jnp.max(got_first[step], axis=0))
            for copy in second_copies(step):
                copy.start()

        halos[2].wait_recv()
        halos[3].wait_recv()
        ghosts(radial_cells, recv_radial, stage, wall, outer, True)
        rim_states(radial_cells, 1)
        faces(radial_cells, 1, radial_rate, 3)

        def turn_back(i, carry):
            block = radial_rate[i, 1 : 1 + TILES].reshape(LANES, LANES)
            turned[i] = block.T.reshape(TILES, ROWS, LANES)
            return carry

        lax.fori_loop(0, 6, turn_back, 0)

        @pl.when(section == 0)
        def _():
            sends = second_copies(step)
            for copy in sends:
                copy.wait_recv()
            top = jnp.maximum(max_second[step], jnp.max(got_second[step], axis=0))
            dt = CFL_NUMBER / jnp.broadcast_to(jnp.max(top, axis=1, keepdims=True), (ROWS, LANES))
            dt_ref[...] = dt
            steps_ref[step] = jnp.max(dt)
            for copy in sends:
                copy.wait_send()
            for copy in first_copies(step):
                copy.wait_send()

        for copy in halos:
            copy.wait_send()

        third = jnp.float32(1.0 / 3.0)
        keep = jnp.where(section == 0, 0.0, jnp.where(section == 1, 0.75, third))
        take = jnp.where(section == 0, 1.0, jnp.where(section == 1, 0.25, jnp.float32(2.0 / 3.0)))
        closing = section == 2
        dt = dt_ref[...]

        def update(r, most):
            for k in range(UPDATES):
                t = r * UPDATES + k
                q_one, q_two, u, v, p, a = (axial_cells[i, GHOST + t] for i in range(6))
                old = [fields[i, t] for i in range(6)]
                over = v * per_radius
                carried = (q_one + q_two) * over
                source = (q_one * over, q_two * over, u * carried, v * carried, (old[4] + p) * over)
                new = []
                for i in range(6):
                    change = axial_rate[i, t + 1] + turned[i, t]
                    if i < 5:
                        change = change - source[i]
                    start = base[i, t]
                    value = keep * start + take * (old[i] + dt * change)
                    fields[i, t] = value
                    base[i, t] = jnp.where(closing, value, start)
                    new.append(value)
                density = new[0] + new[1]
                gamma_sum, stiff_sum = mixture(new[5])
                inverse = 1.0 / (density * gamma_sum)
                per_density = inverse * gamma_sum
                u = new[2] * per_density
                v = new[3] * per_density
                p = (new[4] - 0.5 * (new[2] * u + new[3] * v) - stiff_sum) * (inverse * density)
                for i, value in enumerate((new[0], new[1], u, v, p, new[5])):
                    axial_cells[i, GHOST + t] = value
                speed = jnp.abs(u) + jnp.abs(v) + celerity_of(density, p, gamma_sum, stiff_sum)
                most = jnp.maximum(most, speed)
            return most

        most = lax.fori_loop(0, TILES // UPDATES, update, jnp.zeros((ROWS, LANES), jnp.float32))

        @pl.when(jnp.logical_and(closing, step < STEPS - 1))
        def _():
            max_first[step + 1] = jnp.max(most, axis=0, keepdims=True)
            for copy in first_copies(step + 1):
                copy.start()

        return carry

    lax.fori_loop(0, STAGES, stage_body, 0)

    def finish(t, carry):
        for i, value in enumerate(ambient_cell()):
            moved = jnp.take_along_axis(fields[i, t], from_lanes, axis=1)
            out_ref[i, pl.ds(t, ROWS, stride=TILES), :] = jnp.where(block_first, jnp.float32(value), moved)
        return carry

    lax.fori_loop(0, TILES, finish, 0)


def solution(mesh):
    ax_size, rad_size = mesh.shape["ax"], mesh.shape["rad"]
    sizes = (ax_size // (2 * X_CHIPS), X_CHIPS, 2, rad_size)
    first = sizes[0] * sizes[2] - 1
    second = sizes[1] * sizes[3] - 1

    def shards(labels, jitter):
        block = labels.shape
        f32 = jnp.float32
        tile = (TILES, ROWS, LANES)
        dma = pltpu.SemaphoreType.DMA
        return pl.pallas_call(
            functools.partial(kernel, sizes),
            out_shape=(jax.ShapeDtypeStruct((6, *block), f32), jax.ShapeDtypeStruct((STEPS,), f32)),
            in_specs=[pl.BlockSpec(memory_space=pl.ANY)] * 2,
            out_specs=(pl.BlockSpec(memory_space=pltpu.VMEM), pl.BlockSpec(memory_space=pltpu.SMEM)),
            scratch_shapes=[
                pltpu.VMEM(block, jnp.int32),
                pltpu.VMEM(block, f32),
                pltpu.VMEM(block, jnp.int32),
                pltpu.VMEM(block, f32),
                pltpu.VMEM((6, TILES + 2 * GHOST, ROWS, LANES), f32),
                pltpu.VMEM((6, TILES + 2 * GHOST, ROWS, LANES), f32),
                pltpu.VMEM((6, *tile), f32),
                pltpu.VMEM((6, *tile), f32),
                pltpu.VMEM((2, 6, TILES + 3, ROWS, LANES), f32),
                pltpu.VMEM((2, 6, TILES + 3, ROWS, LANES), f32),
                pltpu.VMEM((6, TILES + 2, ROWS, LANES), f32),
                pltpu.VMEM((6, TILES + 2, ROWS, LANES), f32),
                pltpu.VMEM((6, *tile), f32),
                pltpu.VMEM((ROWS, LANES), f32),
                pltpu.VMEM((2, 18, 1, LANES), f32),
                pltpu.VMEM((2, 18, 1, LANES), f32),
                pltpu.VMEM((STAGES, 2, 18, 1, LANES), f32),
                pltpu.VMEM((STAGES, 2, 18, 1, LANES), f32),
                pltpu.VMEM((STEPS, 1, LANES), f32),
                pltpu.VMEM((STEPS, 1, LANES), f32),
                pltpu.VMEM((STEPS, first, 1, LANES), f32),
                pltpu.VMEM((STEPS, second, 1, LANES), f32),
                dma((2,)),
                dma((2,)),
                dma((2,)),
                dma((STAGES, 4)),
                dma((STAGES, 4)),
                dma((STEPS, first)),
                dma((STEPS, first)),
                dma((STEPS, second)),
                dma((STEPS, second)),
            ],
            compiler_params=pltpu.CompilerParams(collective_id=0, has_side_effects=True),
        )(labels, jitter)

    return jax.shard_map(
        shards, mesh=mesh, in_specs=(P("ax", "rad"),) * 2, out_specs=(P(None, "ax", "rad"), P()), check_vma=False
    )
```

```python
import functools

import jax
import jax.numpy as jnp
from jax import lax
from jax.experimental import pallas as pl
from jax.experimental.pallas import tpu as pltpu
from jax.sharding import PartitionSpec as P

MESH = pl.DeviceIdType.MESH

STEPS = 3
STAGES = 3 * STEPS
X_CHIPS = 4

G_LIQUID = 4.4
PI_LIQUID = 1.0
G_GAS = 1.4
PI_GAS = 0.0
CFL_NUMBER = 0.3
WENO_EPS = 1e-06
ALPHA_TABLE = (0.99, 0.99, 0.01)
LIQUID_TABLE = (1.0, 1.25, 1.0)
GAS_TABLE = (0.1, 0.1, 0.1)
VELOCITY_TABLE = (0.0, 0.4, 0.0)
PRESSURE_TABLE = (1.0, 3.0, 1.0)

GAMMA_GAS = 1.0 / (G_GAS - 1.0)
GAMMA_SLOPE = 1.0 / (G_LIQUID - 1.0) - GAMMA_GAS
STIFF_GAS = G_GAS * PI_GAS / (G_GAS - 1.0)
STIFF_SLOPE = G_LIQUID * PI_LIQUID / (G_LIQUID - 1.0) - STIFF_GAS

TILES = 16
ROWS = 8
LANES = 128
GHOST = 3
FACES = 3
RIMS = 3
VMEM_BYTES = 16 * 2**20
UPDATES = 5
RUN = 6
FINISHED = 4
TURNS = 6


def mixture(fraction):
    gamma_sum = GAMMA_GAS + GAMMA_SLOPE * fraction
    stiff_sum = STIFF_SLOPE * fraction
    if STIFF_GAS != 0.0:
        stiff_sum = stiff_sum + STIFF_GAS
    return gamma_sum, stiff_sum


def initial_cells(labels, jitter):
    def lookup(table):
        return jnp.where(labels == 0, table[0], jnp.where(labels == 1, table[1], table[2]))

    fraction = lookup(ALPHA_TABLE)
    part_one = fraction * lookup(LIQUID_TABLE) * jitter
    part_two = (1.0 - fraction) * lookup(GAS_TABLE) * jitter
    speed = lookup(VELOCITY_TABLE)
    pressure = lookup(PRESSURE_TABLE) * jitter
    return part_one, part_two, speed, pressure, fraction


def ambient_cell():
    fraction = ALPHA_TABLE[0]
    part_one = fraction * LIQUID_TABLE[0]
    part_two = (1.0 - fraction) * GAS_TABLE[0]
    density = part_one + part_two
    speed, pressure = VELOCITY_TABLE[0], PRESSURE_TABLE[0]
    gamma_sum, stiff_sum = mixture(fraction)
    energy = gamma_sum * pressure + stiff_sum + 0.5 * density * speed * speed
    return part_one, part_two, density * speed, 0.0, energy, fraction


def celerity_of(density, pressure, gamma_sum, stiff_sum):
    top = gamma_sum * pressure + stiff_sum + pressure
    return top * lax.rsqrt(top * (gamma_sum * density))


def weno_terms(ea, eb, ec, ed, da, db, dc, ta, tb, tc, ga, gb):
    smooth_zero = ta + eb * (eb + da)
    smooth_one = tb + eb * ec
    smooth_two = tc + ec * (ec - dc)
    square_zero = smooth_zero * smooth_zero
    square_one = smooth_one * smooth_one
    square_two = smooth_two * smooth_two
    weight_zero = square_one * square_two
    weight_one = square_zero * square_two
    weight_two = square_zero * square_one
    low = weight_zero * ga
    high = weight_two * gb
    both = low + high
    twice = both + both
    common = 6.0 * weight_one + (weight_zero + weight_two)
    upper = (twice + high) / (common + (weight_two + weight_two))
    lower = (twice + low) / (common + (weight_zero + weight_zero))
    return upper, lower


def weno_cell(cells):
    m2, m1, c, p1, p2 = cells
    ea, eb, ec, ed = m1 - m2, c - m1, p1 - c, p2 - p1
    da, db, dc = eb - ea, ec - eb, ed - ec
    ta, tb, tc = (d * (d * (4.0 / 3.0)) + WENO_EPS for d in (da, db, dc))
    qa, qb, qc = (d * (1.0 / 6.0) for d in (da, db, dc))
    upper, lower = weno_terms(ea, eb, ec, ed, da, db, dc, ta, tb, tc, qb - qa, qc - qb)
    base = c + (qb + qb)
    return base + 0.5 * eb - upper, base - 0.5 * ec + lower


def weno_run(w, count):
    e = w[1:] - w[:-1]
    d = e[1:] - e[:-1]
    t = d * (d * (4.0 / 3.0)) + WENO_EPS
    q = d * (1.0 / 6.0)
    g = q[1:] - q[:-1]
    n = count
    upper, lower = weno_terms(
        e[:n], e[1 : n + 1], e[2 : n + 2], e[3:], d[:n], d[1 : n + 1], d[2:], t[:n], t[1 : n + 1], t[2:], g[:n], g[1:]
    )
    middle = q[1 : n + 1]
    base = w[2 : n + 2] + (middle + middle)
    return base + 0.5 * e[1 : n + 1] - upper, base - 0.5 * e[2 : n + 2] + lower


def hllc(left, right, normal):
    tangent = 5 - normal

    def side(state):
        density = state[0] + state[1]
        gamma_sum, stiff_sum = mixture(state[5])
        inner = gamma_sum * state[4] + stiff_sum
        top = inner + state[4]
        return density, inner, top * lax.rsqrt(top * (gamma_sum * density))

    rho_l, inner_l, c_l = side(left)
    rho_r, inner_r, c_r = side(right)
    n_l, n_r, p_l, p_r = left[normal], right[normal], left[4], right[4]
    low = jnp.minimum(n_l - c_l, n_r - c_r)
    high = jnp.maximum(n_l + c_l, n_r + c_r)
    mass_l = rho_l * (low - n_l)
    mass_r = rho_r * (high - n_r)
    star = (p_r - p_l + mass_l * n_l - mass_r * n_r) / (mass_l - mass_r)
    forward = star >= 0.0
    outer_left = low >= 0.0
    pick = jnp.logical_or(outer_left, forward)

    def chosen(a, b):
        return jnp.where(pick, a, b)

    q_one, q_two = chosen(left[0], right[0]), chosen(left[1], right[1])
    n, t, p = chosen(n_l, n_r), chosen(left[tangent], right[tangent]), chosen(p_l, p_r)
    wave, mass, inner = chosen(low, high), chosen(mass_l, mass_r), chosen(inner_l, inner_r)
    rho = q_one + q_two
    energy = inner + 0.5 * rho * (n * n + t * t)
    plain = jnp.logical_or(outer_left, jnp.logical_and(jnp.logical_not(pick), high < 0.0))
    inverse = 1.0 / (wave - star)
    factor = (wave - n) * inverse
    jump = star - n
    star_energy = factor * energy + jump * (rho * factor * star + p * inverse)
    star_pressure = p + mass * jump
    speed = jnp.where(plain, n, star)
    scaled = jnp.where(plain, n, factor * star)
    energy = jnp.where(plain, energy, star_energy)
    p = jnp.where(plain, p, star_pressure)
    carried = rho * scaled
    along = carried * speed + p
    across = carried * t
    moments = (along, across) if normal == 2 else (across, along)
    fraction = star * jnp.where(forward, left[5], right[5])
    return [q_one * scaled, q_two * scaled, *moments, (energy + p) * speed, fraction, star]


def kernel(
    sizes,
    labels_hbm,
    jitter_hbm,
    fields,
    steps_ref,
    own_labels,
    own_jitter,
    labels,
    jitter,
    axial_cells,
    radial_cells,
    base,
    upper,
    lower,
    axial_rate,
    radial_rate,
    turned,
    strip,
    strip_rate,
    dt_ref,
    send_axial,
    send_radial,
    recv_axial,
    recv_radial,
    max_first,
    max_second,
    got_first,
    got_second,
    local_sem,
    shift_send,
    shift_recv,
    halo_send,
    halo_recv,
    first_send,
    first_recv,
    second_send,
    second_recv,
):
    z_size, x_size, core_size, rad_size = sizes
    ax_size = z_size * x_size * core_size
    ax, rad = lax.axis_index("ax"), lax.axis_index("rad")
    core = lax.rem(ax, core_size)
    x = lax.rem(lax.div(ax, core_size), x_size)
    z = lax.div(ax, core_size * x_size)

    def at(z, x, core, rad):
        return ((z * x_size + x) * core_size + core, rad)

    first_group = [
        at(lax.rem(z + dz, z_size), x, lax.rem(core + dc, core_size), rad)
        for dz in range(z_size)
        for dc in range(core_size)
        if (dz, dc) != (0, 0)
    ]
    second_group = [
        at(z, lax.rem(x + dx, x_size), core, lax.rem(rad + dr, rad_size))
        for dx in range(x_size)
        for dr in range(rad_size)
        if (dx, dr) != (0, 0)
    ]
    ax_next = (lax.rem(ax + 1, ax_size), rad)
    ax_last = (lax.rem(ax + ax_size - 1, ax_size), rad)
    rad_next = (ax, lax.rem(rad + 1, rad_size))
    rad_last = (ax, lax.rem(rad + rad_size - 1, rad_size))

    block_first = ax == ax_size - 1
    block_last = ax == ax_size - 2
    wall = rad == 0
    outer = rad == rad_size - 1

    lane = lax.broadcasted_iota(jnp.int32, (ROWS, LANES), 1)
    row = lax.broadcasted_iota(jnp.int32, (ROWS, LANES), 0)

    copies = [
        pltpu.make_async_copy(labels_hbm, own_labels, local_sem.at[0]),
        pltpu.make_async_copy(jitter_hbm, own_jitter, local_sem.at[1]),
    ]
    for copy in copies:
        copy.start()
    barrier = pltpu.get_barrier_semaphore()
    greeted = first_group + second_group + [ax_next, ax_last]
    for device in greeted:
        pl.semaphore_signal(barrier, inc=1, device_id=device, device_id_type=MESH)
    for copy in copies:
        copy.wait()

    def first_copies(step):
        return [
            pltpu.make_async_remote_copy(
                src_ref=max_first.at[step],
                dst_ref=got_first.at[step, i],
                send_sem=first_send.at[step, i],
                recv_sem=first_recv.at[step, i],
                device_id=device,
                device_id_type=MESH,
            )
            for i, device in enumerate(first_group)
        ]

    def second_copies(step):
        return [
            pltpu.make_async_remote_copy(
                src_ref=max_second.at[step],
                dst_ref=got_second.at[step, i],
                send_sem=second_send.at[step, i],
                recv_sem=second_recv.at[step, i],
                device_id=device,
                device_id_type=MESH,
            )
            for i, device in enumerate(second_group)
        ]

    def halo_copies(stage, which=(0, 1, 2, 3)):
        parity = lax.rem(stage, 2)
        pairs = [
            (send_axial.at[1], recv_axial.at[stage, 0], ax_next),
            (send_axial.at[0], recv_axial.at[stage, 1], ax_last),
            (send_radial.at[1], recv_radial.at[stage, 0], rad_next),
            (send_radial.at[0], recv_radial.at[stage, 1], rad_last),
        ]
        return [
            pltpu.make_async_remote_copy(
                src_ref=source,
                dst_ref=target,
                send_sem=halo_send.at[parity, i],
                recv_sem=halo_recv.at[parity, i],
                device_id=device,
                device_id_type=MESH,
            )
            for i, (source, target, device) in enumerate(pairs)
            if i in which
        ]

    def own_speed(t, most):
        part_one, part_two, speed, pressure, fraction = initial_cells(
            own_labels[pl.ds(t * ROWS, ROWS), :], own_jitter[pl.ds(t * ROWS, ROWS), :]
        )
        celerity = celerity_of(part_one + part_two, pressure, *mixture(fraction))
        return jnp.maximum(most, jnp.abs(speed) + celerity)

    most = lax.fori_loop(0, TILES, own_speed, jnp.zeros((ROWS, LANES), jnp.float32))
    max_first[0] = jnp.max(most, axis=0, keepdims=True)

    pl.semaphore_wait(barrier, len(greeted))
    for copy in first_copies(0):
        copy.start()
    shifts = [
        pltpu.make_async_remote_copy(
            src_ref=source,
            dst_ref=target,
            send_sem=shift_send.at[i],
            recv_sem=shift_recv.at[i],
            device_id=ax_last,
            device_id_type=MESH,
        )
        for i, (source, target) in enumerate(((labels_hbm, labels), (jitter_hbm, jitter)))
    ]
    for copy in shifts:
        copy.start()
    for copy in shifts:
        copy.wait()

    def second_phase(step):
        for copy in first_copies(step):
            copy.wait_recv()
        max_second[step] = jnp.maximum(max_first[step], jnp.max(got_first[step], axis=0))
        for copy in second_copies(step):
            copy.start()

    second_phase(0)

    to_lanes = (lane % ROWS) * TILES + lane // ROWS
    def start_cells(t, carry):
        rows = pl.ds(t, ROWS, stride=TILES)
        part_one, part_two, speed, pressure, fraction = initial_cells(
            jnp.take_along_axis(labels[rows, :], to_lanes, axis=1), jnp.take_along_axis(jitter[rows, :], to_lanes, axis=1)
        )
        density = part_one + part_two
        gamma_sum, stiff_sum = mixture(fraction)
        still = jnp.zeros_like(density)
        energy = gamma_sum * pressure + stiff_sum + 0.5 * density * speed * speed
        for i, value in enumerate((part_one, part_two, density * speed, still, energy, fraction)):
            fields[i, t] = value
            base[i, t] = value
        for i, value in enumerate((part_one, part_two, speed, still, pressure, fraction)):
            axial_cells[i, GHOST + t] = value
        return carry

    lax.fori_loop(0, TILES, start_cells, 0)

    radius = (rad * LANES + to_lanes).astype(jnp.float32) + 0.5
    per_radius = 1.0 / radius

    def take_rims(cells, send):
        for i in range(6):
            for k in range(GHOST):
                send[0, 3 * i + k] = cells[i, GHOST + k, 0:1, :]
                send[1, 3 * i + k] = cells[i, TILES + k, ROWS - 1 : ROWS, :]

    def wrapped(cells):
        for i in range(6):
            for k in range(GHOST):
                cells[i, k] = pltpu.roll(cells[i, TILES + k], 1, 0)
                cells[i, GHOST + TILES + k] = pltpu.roll(cells[i, GHOST + k], ROWS - 1, 0)

    def own_strip(cells, which):
        for i in range(6):
            q = {2: 3, 3: 2}.get(i, i) if which else i
            for k in range(6):
                strip[q, which, 2 * k + 6 : 2 * k + 7, :] = cells[i, GHOST + k, 0:1, :]
                strip[q, which, 2 * k + 1 : 2 * k + 2, :] = cells[i, GHOST + 10 + k, ROWS - 1 : ROWS, :]

    def rim_strip(recv, stage, which, at_low, at_high):
        for i in range(6):
            q = {2: 3, 3: 2}.get(i, i) if which else i
            high = strip[q, which, 11:12, :]
            for k in range(GHOST):
                if which:
                    low = strip[q, which, 10 - 2 * k : 11 - 2 * k, :]
                    if i == 3:
                        low = -low
                else:
                    low = strip[q, which, 6:7, :]
                strip[q, which, 2 * k : 2 * k + 1, :] = jnp.where(at_low, low, recv[stage, 0, 3 * i + k])
                strip[q, which, 2 * k + 13 : 2 * k + 14, :] = jnp.where(at_high, high, recv[stage, 1, 3 * i + k])

    def strip_rates():
        left, right = [], []
        for i in range(6):
            w = [strip[i, :, 2 * k : 2 * k + 8, :] for k in range(6)]
            left.append(weno_cell(w[:5])[0])
            right.append(weno_cell(w[1:])[1])
            if i == 5:
                fraction = w[3]
        flux = hllc(left, right, 2)
        change = [value - pltpu.roll(value, ROWS - 2, 1) for value in flux]
        change[5] = change[5] - fraction * change[6]
        for i in range(6):
            strip_rate[i] = change[i]
        for i in range(6):
            q = {2: 3, 3: 2}.get(i, i)
            for k in range(GHOST):
                axial_rate[i, 1 + k, 0:1, :] = strip_rate[i, 0, 2 * k : 2 * k + 1, :]
                axial_rate[i, TILES - 2 + k, ROWS - 1 : ROWS, :] = strip_rate[i, 0, 2 * k + 1 : 2 * k + 2, :]
                radial_rate[i, 1 + k, 0:1, :] = strip_rate[q, 1, 2 * k : 2 * k + 1, :]
                radial_rate[i, TILES - 2 + k, ROWS - 1 : ROWS, :] = strip_rate[q, 1, 2 * k + 1 : 2 * k + 2, :]

    def all_states(i, carry):
        for which, cells in enumerate((axial_cells, radial_cells)):
            for first in range(0, TILES + 2, RUN):
                up, down = weno_run(cells[i, first : first + RUN + 4], RUN)
                upper[which, i, first : first + RUN] = up
                lower[which, i, first : first + RUN] = down
        return carry

    def faces(cells, which, rate, normal):
        def some(r, below):
            for k in range(FACES):
                f = r * FACES + k
                above = hllc([upper[which, i, f] for i in range(6)], [lower[which, i, f + 1] for i in range(6)], normal)
                change = [b - a for b, a in zip(below, above)]
                change[5] = change[5] - cells[5, f + 2] * change[6]
                for i in range(6):
                    rate[i, f] = change[i]
                below = tuple(above)
            return below

        lax.fori_loop(0, (TILES + 2) // FACES, some, (jnp.zeros((ROWS, LANES), jnp.float32),) * 7)

    def send_axial_rims(stage):
        take_rims(axial_cells, send_axial)
        for copy in halo_copies(stage, (0, 1)):
            copy.start()

    def send_radial_rims(stage):
        def turn(r, carry):
            for k in range(TURNS):
                i = r * TURNS + k
                block = axial_cells[i, GHOST : GHOST + TILES].reshape(LANES, LANES)
                radial_cells[i, GHOST : GHOST + TILES] = block.T.reshape(TILES, ROWS, LANES)
            return carry

        lax.fori_loop(0, 6 // TURNS, turn, 0)
        take_rims(radial_cells, send_radial)
        for copy in halo_copies(stage, (2, 3)):
            copy.start()

    send_axial_rims(0)
    send_radial_rims(0)

    def stage_body(stage, carry):
        step = lax.div(stage, 3)
        section = stage - 3 * step
        halos = halo_copies(stage)

        wrapped(axial_cells)
        wrapped(radial_cells)
        own_strip(axial_cells, 0)
        own_strip(radial_cells, 1)
        lax.fori_loop(0, 6, all_states, 0)
        faces(axial_cells, 0, axial_rate, 2)
        faces(radial_cells, 1, radial_rate, 3)

        for copy in halos:
            copy.wait_recv()
        rim_strip(recv_axial, stage, 0, block_first, block_last)
        rim_strip(recv_radial, stage, 1, wall, outer)
        strip_rates()

        @pl.when(jnp.logical_and(section == 0, step > 0))
        def _():
            second_phase(step)

        def turn_back(r, carry):
            for k in range(TURNS):
                i = r * TURNS + k
                block = radial_rate[i, 1 : 1 + TILES].reshape(LANES, LANES)
                turned[i] = block.T.reshape(TILES, ROWS, LANES)
            return carry

        lax.fori_loop(0, 6 // TURNS, turn_back, 0)

        @pl.when(section == 0)
        def _():
            sends = second_copies(step)
            for copy in sends:
                copy.wait_recv()
            top = jnp.maximum(max_second[step], jnp.max(got_second[step], axis=0))
            dt = CFL_NUMBER / jnp.broadcast_to(jnp.max(top, axis=1, keepdims=True), (ROWS, LANES))
            dt_ref[...] = dt
            steps_ref[step] = jnp.max(dt)
            for copy in sends:
                copy.wait_send()
            for copy in first_copies(step):
                copy.wait_send()

        for copy in halos:
            copy.wait_send()

        third = jnp.float32(1.0 / 3.0)
        keep = jnp.where(section == 0, 0.0, jnp.where(section == 1, 0.75, third))
        take = jnp.where(section == 0, 1.0, jnp.where(section == 1, 0.25, jnp.float32(2.0 / 3.0)))
        closing = section == 2
        dt = dt_ref[...]

        def update(tiles, most):
            for t in tiles:
                q_one, q_two, u, v, p, a = (axial_cells[i, GHOST + t] for i in range(6))
                old = [fields[i, t] for i in range(6)]
                over = v * per_radius
                carried = (q_one + q_two) * over
                source = (q_one * over, q_two * over, u * carried, v * carried, (old[4] + p) * over)
                new = []
                for i in range(6):
                    change = axial_rate[i, t + 1] + turned[i, t]
                    if i < 5:
                        change = change - source[i]
                    start = base[i, t]
                    value = keep * start + take * (old[i] + dt * change)
                    fields[i, t] = value
                    base[i, t] = jnp.where(closing, value, start)
                    new.append(value)
                density = new[0] + new[1]
                gamma_sum, stiff_sum = mixture(new[5])
                inverse = 1.0 / (density * gamma_sum)
                per_density = inverse * gamma_sum
                u = new[2] * per_density
                v = new[3] * per_density
                p = (new[4] - 0.5 * (new[2] * u + new[3] * v) - stiff_sum) * (inverse * density)
                for i, value in enumerate((new[0], new[1], u, v, p, new[5])):
                    axial_cells[i, GHOST + t] = value
                speed = jnp.abs(u) + jnp.abs(v) + celerity_of(density, p, gamma_sum, stiff_sum)
                most = jnp.maximum(most, speed)
            return most

        most = lax.fori_loop(
            0,
            GHOST // RIMS,
            lambda r, m: update([base_tile + r * RIMS + k for k in range(RIMS) for base_tile in (0, TILES - GHOST)], m),
            jnp.zeros((ROWS, LANES), jnp.float32),
        )

        @pl.when(stage < STAGES - 1)
        def _():
            send_axial_rims(stage + 1)

        most = lax.fori_loop(
            0,
            (TILES - 2 * GHOST) // UPDATES,
            lambda r, m: update([GHOST + r * UPDATES + k for k in range(UPDATES)], m),
            most,
        )

        @pl.when(jnp.logical_and(closing, step < STEPS - 1))
        def _():
            max_first[step + 1] = jnp.max(most, axis=0, keepdims=True)
            for copy in first_copies(step + 1):
                copy.start()

        @pl.when(stage < STAGES - 1)
        def _():
            send_radial_rims(stage + 1)

        return carry

    lax.fori_loop(0, STAGES, stage_body, 0)


def finish(ax_size, fields, steps, out_ref, steps_ref):
    outside = lax.axis_index("ax") == ax_size - 1
    lane = lax.broadcasted_iota(jnp.int32, (ROWS, LANES), 1)
    from_lanes = (lane % TILES) * ROWS + lane // TILES
    for i in range(STEPS):
        steps_ref[i] = steps[i]

    def one(r, carry):
        for k in range(FINISHED):
            t = r * FINISHED + k
            for i, value in enumerate(ambient_cell()):
                moved = jnp.take_along_axis(fields[i, t], from_lanes, axis=1)
                out_ref[i, pl.ds(t, ROWS, stride=TILES), :] = jnp.where(outside, jnp.float32(value), moved)
        return carry

    lax.fori_loop(0, TILES // FINISHED, one, 0)


def solution(mesh):
    ax_size, rad_size = mesh.shape["ax"], mesh.shape["rad"]
    sizes = (ax_size // (2 * X_CHIPS), X_CHIPS, 2, rad_size)
    first = sizes[0] * sizes[2] - 1
    second = sizes[1] * sizes[3] - 1

    def shards(labels, jitter):
        block = labels.shape
        f32 = jnp.float32
        tile = (TILES, ROWS, LANES)
        dma = pltpu.SemaphoreType.DMA
        labels, jitter = (pltpu.with_memory_space_constraint(a, pltpu.HBM) for a in (labels, jitter))
        fields, steps = pl.pallas_call(
            functools.partial(kernel, sizes),
            out_shape=(jax.ShapeDtypeStruct((6, *tile), f32), jax.ShapeDtypeStruct((STEPS,), f32)),
            in_specs=[pl.BlockSpec(memory_space=pltpu.HBM)] * 2,
            out_specs=(pl.BlockSpec(memory_space=pltpu.VMEM), pl.BlockSpec(memory_space=pltpu.SMEM)),
            scratch_shapes=[
                pltpu.VMEM(block, jnp.int32),
                pltpu.VMEM(block, f32),
                pltpu.VMEM(block, jnp.int32),
                pltpu.VMEM(block, f32),
                pltpu.VMEM((6, TILES + 2 * GHOST, ROWS, LANES), f32),
                pltpu.VMEM((6, TILES + 2 * GHOST, ROWS, LANES), f32),
                pltpu.VMEM((6, *tile), f32),
                pltpu.VMEM((2, 6, TILES + 3, ROWS, LANES), f32),
                pltpu.VMEM((2, 6, TILES + 3, ROWS, LANES), f32),
                pltpu.VMEM((6, TILES + 2, ROWS, LANES), f32),
                pltpu.VMEM((6, TILES + 2, ROWS, LANES), f32),
                pltpu.VMEM((6, *tile), f32),
                pltpu.VMEM((6, 2, 24, LANES), f32),
                pltpu.VMEM((6, 2, ROWS, LANES), f32),
                pltpu.VMEM((ROWS, LANES), f32),
                pltpu.VMEM((2, 18, 1, LANES), f32),
                pltpu.VMEM((2, 18, 1, LANES), f32),
                pltpu.VMEM((STAGES, 2, 18, 1, LANES), f32),
                pltpu.VMEM((STAGES, 2, 18, 1, LANES), f32),
                pltpu.VMEM((STEPS, 1, LANES), f32),
                pltpu.VMEM((STEPS, 1, LANES), f32),
                pltpu.VMEM((STEPS, first, 1, LANES), f32),
                pltpu.VMEM((STEPS, second, 1, LANES), f32),
                dma((2,)),
                dma((2,)),
                dma((2,)),
                dma((2, 4)),
                dma((2, 4)),
                dma((STEPS, first)),
                dma((STEPS, first)),
                dma((STEPS, second)),
                dma((STEPS, second)),
            ],
            compiler_params=pltpu.CompilerParams(
                collective_id=0, has_side_effects=True, vmem_limit_bytes=VMEM_BYTES
            ),
        )(labels, jitter)
        return pl.pallas_call(
            functools.partial(finish, ax_size),
            out_shape=(jax.ShapeDtypeStruct((6, *block), f32), jax.ShapeDtypeStruct((STEPS,), f32)),
            in_specs=[pl.BlockSpec(memory_space=pltpu.VMEM), pl.BlockSpec(memory_space=pltpu.SMEM)],
            out_specs=(pl.BlockSpec(memory_space=pltpu.VMEM), pl.BlockSpec(memory_space=pltpu.SMEM)),
            compiler_params=pltpu.CompilerParams(vmem_limit_bytes=VMEM_BYTES),
        )(fields, steps)

    return jax.shard_map(
        shards, mesh=mesh, in_specs=(P("ax", "rad"),) * 2, out_specs=(P(None, "ax", "rad"), P()), check_vma=False
    )
```

```python
import functools

import jax
import jax.numpy as jnp
from jax import lax
from jax.experimental import pallas as pl
from jax.experimental.pallas import tpu as pltpu
from jax.sharding import PartitionSpec as P

MESH = pl.DeviceIdType.MESH

STEPS = 3
STAGES = 3 * STEPS
X_CHIPS = 4

G_LIQUID = 4.4
PI_LIQUID = 1.0
G_GAS = 1.4
PI_GAS = 0.0
CFL_NUMBER = 0.3
WENO_EPS = 1e-06
ALPHA_TABLE = (0.99, 0.99, 0.01)
LIQUID_TABLE = (1.0, 1.25, 1.0)
GAS_TABLE = (0.1, 0.1, 0.1)
VELOCITY_TABLE = (0.0, 0.4, 0.0)
PRESSURE_TABLE = (1.0, 3.0, 1.0)

GAMMA_GAS = 1.0 / (G_GAS - 1.0)
GAMMA_SLOPE = 1.0 / (G_LIQUID - 1.0) - GAMMA_GAS
STIFF_GAS = G_GAS * PI_GAS / (G_GAS - 1.0)
STIFF_SLOPE = G_LIQUID * PI_LIQUID / (G_LIQUID - 1.0) - STIFF_GAS

TILES = 16
ROWS = 8
LANES = 128
GHOST = 3
FACES = 3
RIMS = 3
VMEM_BYTES = 16 * 2**20
UPDATES = 5
RUN = 6
FINISHED = 4
TURNS = 6


def mixture(fraction):
    gamma_sum = GAMMA_GAS + GAMMA_SLOPE * fraction
    stiff_sum = STIFF_SLOPE * fraction
    if STIFF_GAS != 0.0:
        stiff_sum = stiff_sum + STIFF_GAS
    return gamma_sum, stiff_sum


def initial_cells(labels, jitter):
    def lookup(table):
        return jnp.where(labels == 0, table[0], jnp.where(labels == 1, table[1], table[2]))

    fraction = lookup(ALPHA_TABLE)
    part_one = fraction * lookup(LIQUID_TABLE) * jitter
    part_two = (1.0 - fraction) * lookup(GAS_TABLE) * jitter
    speed = lookup(VELOCITY_TABLE)
    pressure = lookup(PRESSURE_TABLE) * jitter
    return part_one, part_two, speed, pressure, fraction


def ambient_cell():
    fraction = ALPHA_TABLE[0]
    part_one = fraction * LIQUID_TABLE[0]
    part_two = (1.0 - fraction) * GAS_TABLE[0]
    density = part_one + part_two
    speed, pressure = VELOCITY_TABLE[0], PRESSURE_TABLE[0]
    gamma_sum, stiff_sum = mixture(fraction)
    energy = gamma_sum * pressure + stiff_sum + 0.5 * density * speed * speed
    return part_one, part_two, density * speed, 0.0, energy, fraction


def celerity_of(density, pressure, gamma_sum, stiff_sum):
    top = gamma_sum * pressure + stiff_sum + pressure
    return top * lax.rsqrt(top * (gamma_sum * density))


def weno_terms(ea, eb, ec, ed, da, db, dc, ta, tb, tc, ga, gb):
    smooth_zero = ta + eb * (eb + da)
    smooth_one = tb + eb * ec
    smooth_two = tc + ec * (ec - dc)
    square_zero = smooth_zero * smooth_zero
    square_one = smooth_one * smooth_one
    square_two = smooth_two * smooth_two
    weight_zero = square_one * square_two
    weight_one = square_zero * square_two
    weight_two = square_zero * square_one
    low = weight_zero * ga
    high = weight_two * gb
    both = low + high
    twice = both + both
    common = 6.0 * weight_one + (weight_zero + weight_two)
    upper = (twice + high) / (common + (weight_two + weight_two))
    lower = (twice + low) / (common + (weight_zero + weight_zero))
    return upper, lower


def weno_cell(cells):
    m2, m1, c, p1, p2 = cells
    ea, eb, ec, ed = m1 - m2, c - m1, p1 - c, p2 - p1
    da, db, dc = eb - ea, ec - eb, ed - ec
    ta, tb, tc = (d * (d * (4.0 / 3.0)) + WENO_EPS for d in (da, db, dc))
    qa, qb, qc = (d * (1.0 / 6.0) for d in (da, db, dc))
    upper, lower = weno_terms(ea, eb, ec, ed, da, db, dc, ta, tb, tc, qb - qa, qc - qb)
    base = c + (qb + qb)
    return base + 0.5 * eb - upper, base - 0.5 * ec + lower


def weno_run(w, count):
    e = w[1:] - w[:-1]
    d = e[1:] - e[:-1]
    t = d * (d * (4.0 / 3.0)) + WENO_EPS
    q = d * (1.0 / 6.0)
    g = q[1:] - q[:-1]
    n = count
    upper, lower = weno_terms(
        e[:n], e[1 : n + 1], e[2 : n + 2], e[3:], d[:n], d[1 : n + 1], d[2:], t[:n], t[1 : n + 1], t[2:], g[:n], g[1:]
    )
    middle = q[1 : n + 1]
    base = w[2 : n + 2] + (middle + middle)
    return base + 0.5 * e[1 : n + 1] - upper, base - 0.5 * e[2 : n + 2] + lower


def hllc(left, right, normal):
    tangent = 5 - normal

    def side(state):
        density = state[0] + state[1]
        gamma_sum, stiff_sum = mixture(state[5])
        inner = gamma_sum * state[4] + stiff_sum
        top = inner + state[4]
        return density, inner, top * lax.rsqrt(top * (gamma_sum * density))

    rho_l, inner_l, c_l = side(left)
    rho_r, inner_r, c_r = side(right)
    n_l, n_r, p_l, p_r = left[normal], right[normal], left[4], right[4]
    low = jnp.minimum(n_l - c_l, n_r - c_r)
    high = jnp.maximum(n_l + c_l, n_r + c_r)
    mass_l = rho_l * (low - n_l)
    mass_r = rho_r * (high - n_r)
    star = (p_r - p_l + mass_l * n_l - mass_r * n_r) / (mass_l - mass_r)
    forward = star >= 0.0
    outer_left = low >= 0.0
    pick = jnp.logical_or(outer_left, forward)

    def chosen(a, b):
        return jnp.where(pick, a, b)

    q_one, q_two = chosen(left[0], right[0]), chosen(left[1], right[1])
    n, t, p = chosen(n_l, n_r), chosen(left[tangent], right[tangent]), chosen(p_l, p_r)
    wave, mass, inner = chosen(low, high), chosen(mass_l, mass_r), chosen(inner_l, inner_r)
    rho = q_one + q_two
    energy = inner + 0.5 * rho * (n * n + t * t)
    plain = jnp.logical_or(outer_left, jnp.logical_and(jnp.logical_not(pick), high < 0.0))
    inverse = 1.0 / (wave - star)
    factor = (wave - n) * inverse
    jump = star - n
    star_energy = factor * energy + jump * (rho * factor * star + p * inverse)
    star_pressure = p + mass * jump
    speed = jnp.where(plain, n, star)
    scaled = jnp.where(plain, n, factor * star)
    energy = jnp.where(plain, energy, star_energy)
    p = jnp.where(plain, p, star_pressure)
    carried = rho * scaled
    along = carried * speed + p
    across = carried * t
    moments = (along, across) if normal == 2 else (across, along)
    fraction = star * jnp.where(forward, left[5], right[5])
    return [q_one * scaled, q_two * scaled, *moments, (energy + p) * speed, fraction, star]


def far_first(size):
    return sorted(range(size), key=lambda d: -min(d, size - d))


def kernel(
    sizes,
    labels_hbm,
    jitter_hbm,
    fields,
    steps_ref,
    own_labels,
    own_jitter,
    labels,
    jitter,
    axial_cells,
    radial_cells,
    base,
    upper,
    lower,
    axial_rate,
    radial_rate,
    turned,
    total,
    strip,
    strip_rate,
    dt_ref,
    send_axial,
    send_radial,
    recv_axial,
    recv_radial,
    max_first,
    max_second,
    got_first,
    got_second,
    local_sem,
    shift_send,
    shift_recv,
    halo_send,
    halo_recv,
    first_send,
    first_recv,
    second_send,
    second_recv,
):
    z_size, x_size, core_size, rad_size = sizes
    ax_size = z_size * x_size * core_size
    ax, rad = lax.axis_index("ax"), lax.axis_index("rad")
    core = lax.rem(ax, core_size)
    x = lax.rem(lax.div(ax, core_size), x_size)
    z = lax.div(ax, core_size * x_size)

    def at(z, x, core, rad):
        return ((z * x_size + x) * core_size + core, rad)

    first_group = [
        at(lax.rem(z + dz, z_size), x, lax.rem(core + dc, core_size), rad)
        for dz in far_first(z_size)
        for dc in range(core_size)
        if (dz, dc) != (0, 0)
    ]
    second_group = [
        at(z, lax.rem(x + dx, x_size), core, lax.rem(rad + dr, rad_size))
        for dx in far_first(x_size)
        for dr in far_first(rad_size)
        if (dx, dr) != (0, 0)
    ]
    ax_next = (lax.rem(ax + 1, ax_size), rad)
    ax_last = (lax.rem(ax + ax_size - 1, ax_size), rad)
    rad_next = (ax, lax.rem(rad + 1, rad_size))
    rad_last = (ax, lax.rem(rad + rad_size - 1, rad_size))

    block_first = ax == ax_size - 1
    block_last = ax == ax_size - 2
    wall = rad == 0
    outer = rad == rad_size - 1

    lane = lax.broadcasted_iota(jnp.int32, (ROWS, LANES), 1)
    row = lax.broadcasted_iota(jnp.int32, (ROWS, LANES), 0)

    copies = [
        pltpu.make_async_copy(labels_hbm, own_labels, local_sem.at[0]),
        pltpu.make_async_copy(jitter_hbm, own_jitter, local_sem.at[1]),
    ]
    for copy in copies:
        copy.start()
    barrier = pltpu.get_barrier_semaphore()
    greeted = first_group + second_group + [ax_next, ax_last]
    for device in greeted:
        pl.semaphore_signal(barrier, inc=1, device_id=device, device_id_type=MESH)
    for copy in copies:
        copy.wait()

    def first_copies(step):
        return [
            pltpu.make_async_remote_copy(
                src_ref=max_first.at[step],
                dst_ref=got_first.at[step, i],
                send_sem=first_send.at[step],
                recv_sem=first_recv.at[step],
                device_id=device,
                device_id_type=MESH,
            )
            for i, device in enumerate(first_group)
        ]

    def second_copies(step):
        return [
            pltpu.make_async_remote_copy(
                src_ref=max_second.at[step],
                dst_ref=got_second.at[step, i],
                send_sem=second_send.at[step],
                recv_sem=second_recv.at[step],
                device_id=device,
                device_id_type=MESH,
            )
            for i, device in enumerate(second_group)
        ]

    def whole_phase(step, second):
        got, send, recv, group = (
            (got_second, second_send, second_recv, second_group) if second else (got_first, first_send, first_recv, first_group)
        )
        return pltpu.make_async_remote_copy(
            src_ref=got.at[step],
            dst_ref=got.at[step],
            send_sem=send.at[step],
            recv_sem=recv.at[step],
            device_id=group[0],
            device_id_type=MESH,
        )

    def halo_copies(stage, which=(0, 1, 2, 3)):
        parity = lax.rem(stage, 2)
        pairs = [
            (send_axial.at[1], recv_axial.at[stage, 0], ax_next),
            (send_axial.at[0], recv_axial.at[stage, 1], ax_last),
            (send_radial.at[1], recv_radial.at[stage, 0], rad_next),
            (send_radial.at[0], recv_radial.at[stage, 1], rad_last),
        ]
        return [
            pltpu.make_async_remote_copy(
                src_ref=source,
                dst_ref=target,
                send_sem=halo_send.at[parity, i],
                recv_sem=halo_recv.at[parity, i],
                device_id=device,
                device_id_type=MESH,
            )
            for i, (source, target, device) in enumerate(pairs)
            if i in which
        ]

    def own_speed(t, most):
        part_one, part_two, speed, pressure, fraction = initial_cells(
            own_labels[pl.ds(t * ROWS, ROWS), :], own_jitter[pl.ds(t * ROWS, ROWS), :]
        )
        celerity = celerity_of(part_one + part_two, pressure, *mixture(fraction))
        return jnp.maximum(most, jnp.abs(speed) + celerity)

    most = lax.fori_loop(0, TILES, own_speed, jnp.zeros((ROWS, LANES), jnp.float32))
    max_first[0] = jnp.max(most, axis=0, keepdims=True)

    pl.semaphore_wait(barrier, len(greeted))
    for copy in first_copies(0):
        copy.start()
    shifts = [
        pltpu.make_async_remote_copy(
            src_ref=source,
            dst_ref=target,
            send_sem=shift_send.at[i],
            recv_sem=shift_recv.at[i],
            device_id=ax_last,
            device_id_type=MESH,
        )
        for i, (source, target) in enumerate(((labels_hbm, labels), (jitter_hbm, jitter)))
    ]
    for copy in shifts:
        copy.start()
    for copy in shifts:
        copy.wait()

    def second_phase(step):
        whole_phase(step, False).wait_recv()
        max_second[step] = jnp.maximum(max_first[step], jnp.max(got_first[step], axis=0))
        for copy in second_copies(step):
            copy.start()

    second_phase(0)

    to_lanes = (lane % ROWS) * TILES + lane // ROWS
    def start_cells(t, carry):
        rows = pl.ds(t, ROWS, stride=TILES)
        part_one, part_two, speed, pressure, fraction = initial_cells(
            jnp.take_along_axis(labels[rows, :], to_lanes, axis=1), jnp.take_along_axis(jitter[rows, :], to_lanes, axis=1)
        )
        density = part_one + part_two
        gamma_sum, stiff_sum = mixture(fraction)
        still = jnp.zeros_like(density)
        energy = gamma_sum * pressure + stiff_sum + 0.5 * density * speed * speed
        for i, value in enumerate((part_one, part_two, density * speed, still, energy, fraction)):
            fields[i, t] = value
            base[i, t] = value
        for i, value in enumerate((part_one, part_two, speed, still, pressure, fraction)):
            axial_cells[i, GHOST + t] = value
        return carry

    lax.fori_loop(0, TILES, start_cells, 0)

    radius = (rad * LANES + to_lanes).astype(jnp.float32) + 0.5
    per_radius = 1.0 / radius

    def take_rims(cells, send):
        for i in range(6):
            for k in range(GHOST):
                send[0, 3 * i + k] = cells[i, GHOST + k, 0:1, :]
                send[1, 3 * i + k] = cells[i, TILES + k, ROWS - 1 : ROWS, :]

    def wrapped(cells):
        for i in range(6):
            for k in range(GHOST):
                cells[i, k] = pltpu.roll(cells[i, TILES + k], 1, 0)
                cells[i, GHOST + TILES + k] = pltpu.roll(cells[i, GHOST + k], ROWS - 1, 0)

    def own_strip(cells, which):
        for i in range(6):
            q = {2: 3, 3: 2}.get(i, i) if which else i
            for k in range(6):
                strip[q, which, 2 * k + 6 : 2 * k + 7, :] = cells[i, GHOST + k, 0:1, :]
                strip[q, which, 2 * k + 1 : 2 * k + 2, :] = cells[i, GHOST + 10 + k, ROWS - 1 : ROWS, :]

    def rim_strip(recv, stage, which, at_low, at_high):
        for i in range(6):
            q = {2: 3, 3: 2}.get(i, i) if which else i
            high = strip[q, which, 11:12, :]
            for k in range(GHOST):
                if which:
                    low = strip[q, which, 10 - 2 * k : 11 - 2 * k, :]
                    if i == 3:
                        low = -low
                else:
                    low = strip[q, which, 6:7, :]
                strip[q, which, 2 * k : 2 * k + 1, :] = jnp.where(at_low, low, recv[stage, 0, 3 * i + k])
                strip[q, which, 2 * k + 13 : 2 * k + 14, :] = jnp.where(at_high, high, recv[stage, 1, 3 * i + k])

    def strip_rates():
        left, right = [], []
        for i in range(6):
            w = [strip[i, :, 2 * k : 2 * k + 8, :] for k in range(6)]
            left.append(weno_cell(w[:5])[0])
            right.append(weno_cell(w[1:])[1])
            if i == 5:
                fraction = w[3]
        flux = hllc(left, right, 2)
        change = [value - pltpu.roll(value, ROWS - 2, 1) for value in flux]
        change[5] = change[5] - fraction * change[6]
        for i in range(6):
            strip_rate[i] = change[i]
        for i in range(6):
            q = {2: 3, 3: 2}.get(i, i)
            for k in range(GHOST):
                axial_rate[i, 1 + k, 0:1, :] = strip_rate[i, 0, 2 * k : 2 * k + 1, :]
                axial_rate[i, TILES - 2 + k, ROWS - 1 : ROWS, :] = strip_rate[i, 0, 2 * k + 1 : 2 * k + 2, :]
                radial_rate[i, 1 + k, 0:1, :] = strip_rate[q, 1, 2 * k : 2 * k + 1, :]
                radial_rate[i, TILES - 2 + k, ROWS - 1 : ROWS, :] = strip_rate[q, 1, 2 * k + 1 : 2 * k + 2, :]

    def all_states(i, carry):
        for which, cells in enumerate((axial_cells, radial_cells)):
            for first in range(0, TILES + 2, RUN):
                up, down = weno_run(cells[i, first : first + RUN + 4], RUN)
                upper[which, i, first : first + RUN] = up
                lower[which, i, first : first + RUN] = down
        return carry

    def faces(cells, which, rate, normal):
        def some(r, below):
            for k in range(FACES):
                f = r * FACES + k
                above = hllc([upper[which, i, f] for i in range(6)], [lower[which, i, f + 1] for i in range(6)], normal)
                change = [b - a for b, a in zip(below, above)]
                change[5] = change[5] - cells[5, f + 2] * change[6]
                for i in range(6):
                    rate[i, f] = change[i]
                below = tuple(above)
            return below

        lax.fori_loop(0, (TILES + 2) // FACES, some, (jnp.zeros((ROWS, LANES), jnp.float32),) * 7)

    def send_axial_rims(stage, cells=axial_cells):
        take_rims(cells, send_axial)
        for copy in halo_copies(stage, (0, 1)):
            copy.start()

    def turn_cells(axial, radial):
        def turn(r, carry):
            for k in range(TURNS):
                i = r * TURNS + k
                block = axial[i, GHOST : GHOST + TILES].reshape(LANES, LANES)
                radial[i, GHOST : GHOST + TILES] = block.T.reshape(TILES, ROWS, LANES)
            return carry

        lax.fori_loop(0, 6 // TURNS, turn, 0)

    def send_radial_rims(stage, cells=radial_cells):
        take_rims(cells, send_radial)
        for copy in halo_copies(stage, (2, 3)):
            copy.start()

    def whole_rate(t, q_one, q_two, u, v, p, a, energy):
        over = v * per_radius
        carried = (q_one + q_two) * over
        source = (q_one * over, q_two * over, u * carried, v * carried, (energy + p) * over)
        change = [axial_rate[i, t + 1] + turned[i, t] for i in range(6)]
        return [change[i] - source[i] for i in range(5)] + [change[5]]

    def primitives(fields):
        density = fields[0] + fields[1]
        gamma_sum, stiff_sum = mixture(fields[5])
        inverse = 1.0 / (density * gamma_sum)
        per_density = inverse * gamma_sum
        u = fields[2] * per_density
        v = fields[3] * per_density
        p = (fields[4] - 0.5 * (fields[2] * u + fields[3] * v) - stiff_sum) * (inverse * density)
        return fields[0], fields[1], u, v, p, fields[5]

    def advance_rims(recv, stage):
        dt = dt_ref[0:1, :]
        for side in range(2):
            old = [recv[stage - 1, side, 3 * i : 3 * i + 3] for i in range(6)]
            change = [recv[stage, side, 3 * i : 3 * i + 3] for i in range(6)]
            q_one, q_two, u, v, p, a = old
            density = q_one + q_two
            gamma_sum, stiff_sum = mixture(a)
            energy = gamma_sum * p + stiff_sum + 0.5 * density * (u * u + v * v)
            before = (q_one, q_two, density * u, density * v, energy, a)
            for i, value in enumerate(primitives([b + dt * c for b, c in zip(before, change)])):
                recv[stage, side, 3 * i : 3 * i + 3] = value

    send_axial_rims(0)
    turn_cells(axial_cells, radial_cells)
    send_radial_rims(0)

    def stage_body(stage, carry):
        step = lax.div(stage, 3)
        section = stage - 3 * step
        halos = halo_copies(stage)

        wrapped(axial_cells)
        wrapped(radial_cells)
        own_strip(axial_cells, 0)
        own_strip(radial_cells, 1)
        lax.fori_loop(0, 6, all_states, 0)
        faces(axial_cells, 0, axial_rate, 2)
        faces(radial_cells, 1, radial_rate, 3)

        for copy in halos:
            copy.wait_recv()

        @pl.when(section == 1)
        def _():
            advance_rims(recv_axial, stage)
            advance_rims(recv_radial, stage)

        rim_strip(recv_axial, stage, 0, block_first, block_last)
        rim_strip(recv_radial, stage, 1, wall, outer)
        strip_rates()

        @pl.when(jnp.logical_and(section == 0, step > 0))
        def _():
            second_phase(step)

        def turn_back(r, carry):
            for k in range(TURNS):
                i = r * TURNS + k
                block = radial_rate[i, 1 : 1 + TILES].reshape(LANES, LANES)
                turned[i] = block.T.reshape(TILES, ROWS, LANES)
            return carry

        lax.fori_loop(0, 6 // TURNS, turn_back, 0)

        for copy in halos:
            copy.wait_send()

        @pl.when(section == 0)
        def _():
            def rates(t, carry):
                for i, value in enumerate(whole_rate(t, *(axial_cells[i, GHOST + t] for i in range(6)), fields[4, t])):
                    total[0, i, GHOST + t] = value
                return carry

            lax.fori_loop(0, TILES, rates, 0)
            send_axial_rims(stage + 1, total.at[0])
            turn_cells(total.at[0], total.at[1])
            send_radial_rims(stage + 1, total.at[1])
            whole_phase(step, True).wait_recv()
            top = jnp.maximum(max_second[step], jnp.max(got_second[step], axis=0))
            dt = CFL_NUMBER / jnp.broadcast_to(jnp.max(top, axis=1, keepdims=True), (ROWS, LANES))
            dt_ref[...] = dt
            steps_ref[step] = jnp.max(dt)
            whole_phase(step, True).wait_send()
            whole_phase(step, False).wait_send()

        third = jnp.float32(1.0 / 3.0)
        keep = jnp.where(section == 0, 0.0, jnp.where(section == 1, 0.75, third))
        take = jnp.where(section == 0, 1.0, jnp.where(section == 1, 0.25, jnp.float32(2.0 / 3.0)))
        closing = section == 2
        dt = dt_ref[...]

        def update(tiles, most):
            for t in tiles:
                old = [fields[i, t] for i in range(6)]
                change = whole_rate(t, *(axial_cells[i, GHOST + t] for i in range(6)), old[4])
                new = []
                for i in range(6):
                    start = base[i, t]
                    value = keep * start + take * (old[i] + dt * change[i])
                    fields[i, t] = value
                    base[i, t] = jnp.where(closing, value, start)
                    new.append(value)
                q_one, q_two, u, v, p, a = primitives(new)
                for i, value in enumerate((q_one, q_two, u, v, p, a)):
                    axial_cells[i, GHOST + t] = value
                density = q_one + q_two
                gamma_sum, stiff_sum = mixture(a)
                speed = jnp.abs(u) + jnp.abs(v) + celerity_of(density, p, gamma_sum, stiff_sum)
                most = jnp.maximum(most, speed)
            return most

        most = lax.fori_loop(
            0,
            GHOST // RIMS,
            lambda r, m: update([base_tile + r * RIMS + k for k in range(RIMS) for base_tile in (0, TILES - GHOST)], m),
            jnp.zeros((ROWS, LANES), jnp.float32),
        )

        @pl.when(jnp.logical_and(section > 0, stage < STAGES - 1))
        def _():
            send_axial_rims(stage + 1)

        most = lax.fori_loop(
            0,
            (TILES - 2 * GHOST) // UPDATES,
            lambda r, m: update([GHOST + r * UPDATES + k for k in range(UPDATES)], m),
            most,
        )

        @pl.when(jnp.logical_and(closing, step < STEPS - 1))
        def _():
            max_first[step + 1] = jnp.max(most, axis=0, keepdims=True)
            for copy in first_copies(step + 1):
                copy.start()

        @pl.when(stage < STAGES - 1)
        def _():
            turn_cells(axial_cells, radial_cells)

        @pl.when(jnp.logical_and(section > 0, stage < STAGES - 1))
        def _():
            send_radial_rims(stage + 1)

        return carry

    lax.fori_loop(0, STAGES, stage_body, 0)


def finish(ax_size, fields, steps, out_ref, steps_ref):
    outside = lax.axis_index("ax") == ax_size - 1
    lane = lax.broadcasted_iota(jnp.int32, (ROWS, LANES), 1)
    from_lanes = (lane % TILES) * ROWS + lane // TILES
    for i in range(STEPS):
        steps_ref[i] = steps[i]

    def one(r, carry):
        for k in range(FINISHED):
            t = r * FINISHED + k
            for i, value in enumerate(ambient_cell()):
                moved = jnp.take_along_axis(fields[i, t], from_lanes, axis=1)
                out_ref[i, pl.ds(t, ROWS, stride=TILES), :] = jnp.where(outside, jnp.float32(value), moved)
        return carry

    lax.fori_loop(0, TILES // FINISHED, one, 0)


def solution(mesh):
    ax_size, rad_size = mesh.shape["ax"], mesh.shape["rad"]
    sizes = (ax_size // (2 * X_CHIPS), X_CHIPS, 2, rad_size)
    first = sizes[0] * sizes[2] - 1
    second = sizes[1] * sizes[3] - 1

    def shards(labels, jitter):
        block = labels.shape
        f32 = jnp.float32
        tile = (TILES, ROWS, LANES)
        dma = pltpu.SemaphoreType.DMA
        labels, jitter = (pltpu.with_memory_space_constraint(a, pltpu.HBM) for a in (labels, jitter))
        fields, steps = pl.pallas_call(
            functools.partial(kernel, sizes),
            out_shape=(jax.ShapeDtypeStruct((6, *tile), f32), jax.ShapeDtypeStruct((STEPS,), f32)),
            in_specs=[pl.BlockSpec(memory_space=pltpu.HBM)] * 2,
            out_specs=(pl.BlockSpec(memory_space=pltpu.VMEM), pl.BlockSpec(memory_space=pltpu.SMEM)),
            scratch_shapes=[
                pltpu.VMEM(block, jnp.int32),
                pltpu.VMEM(block, f32),
                pltpu.VMEM(block, jnp.int32),
                pltpu.VMEM(block, f32),
                pltpu.VMEM((6, TILES + 2 * GHOST, ROWS, LANES), f32),
                pltpu.VMEM((6, TILES + 2 * GHOST, ROWS, LANES), f32),
                pltpu.VMEM((6, *tile), f32),
                pltpu.VMEM((2, 6, TILES + 3, ROWS, LANES), f32),
                pltpu.VMEM((2, 6, TILES + 3, ROWS, LANES), f32),
                pltpu.VMEM((6, TILES + 2, ROWS, LANES), f32),
                pltpu.VMEM((6, TILES + 2, ROWS, LANES), f32),
                pltpu.VMEM((6, *tile), f32),
                pltpu.VMEM((2, 6, TILES + 2 * GHOST, ROWS, LANES), f32),
                pltpu.VMEM((6, 2, 24, LANES), f32),
                pltpu.VMEM((6, 2, ROWS, LANES), f32),
                pltpu.VMEM((ROWS, LANES), f32),
                pltpu.VMEM((2, 18, 1, LANES), f32),
                pltpu.VMEM((2, 18, 1, LANES), f32),
                pltpu.VMEM((STAGES, 2, 18, 1, LANES), f32),
                pltpu.VMEM((STAGES, 2, 18, 1, LANES), f32),
                pltpu.VMEM((STEPS, 1, LANES), f32),
                pltpu.VMEM((STEPS, 1, LANES), f32),
                pltpu.VMEM((STEPS, first, 1, LANES), f32),
                pltpu.VMEM((STEPS, second, 1, LANES), f32),
                dma((2,)),
                dma((2,)),
                dma((2,)),
                dma((2, 4)),
                dma((2, 4)),
                dma((STEPS,)),
                dma((STEPS,)),
                dma((STEPS,)),
                dma((STEPS,)),
            ],
            compiler_params=pltpu.CompilerParams(
                collective_id=0, has_side_effects=True, vmem_limit_bytes=VMEM_BYTES
            ),
        )(labels, jitter)
        return pl.pallas_call(
            functools.partial(finish, ax_size),
            out_shape=(jax.ShapeDtypeStruct((6, *block), f32), jax.ShapeDtypeStruct((STEPS,), f32)),
            in_specs=[pl.BlockSpec(memory_space=pltpu.VMEM), pl.BlockSpec(memory_space=pltpu.SMEM)],
            out_specs=(pl.BlockSpec(memory_space=pltpu.VMEM), pl.BlockSpec(memory_space=pltpu.SMEM)),
            compiler_params=pltpu.CompilerParams(vmem_limit_bytes=VMEM_BYTES),
        )(fields, steps)

    return jax.shard_map(
        shards, mesh=mesh, in_specs=(P("ax", "rad"),) * 2, out_specs=(P(None, "ax", "rad"), P()), check_vma=False
    )
```

```python
import functools

import jax
import jax.numpy as jnp
from jax import lax
from jax.experimental import pallas as pl
from jax.experimental.pallas import tpu as pltpu
from jax.sharding import PartitionSpec as P

MESH = pl.DeviceIdType.MESH

STEPS = 3
STAGES = 3 * STEPS
X_CHIPS = 4

G_LIQUID = 4.4
PI_LIQUID = 1.0
G_GAS = 1.4
PI_GAS = 0.0
CFL_NUMBER = 0.3
WENO_EPS = 1e-06
ALPHA_TABLE = (0.99, 0.99, 0.01)
LIQUID_TABLE = (1.0, 1.25, 1.0)
GAS_TABLE = (0.1, 0.1, 0.1)
VELOCITY_TABLE = (0.0, 0.4, 0.0)
PRESSURE_TABLE = (1.0, 3.0, 1.0)

GAMMA_GAS = 1.0 / (G_GAS - 1.0)
GAMMA_SLOPE = 1.0 / (G_LIQUID - 1.0) - GAMMA_GAS
STIFF_GAS = G_GAS * PI_GAS / (G_GAS - 1.0)
STIFF_SLOPE = G_LIQUID * PI_LIQUID / (G_LIQUID - 1.0) - STIFF_GAS

TILES = 16
ROWS = 8
LANES = 128
GHOST = 3
FACES = 3
RIMS = 3
VMEM_BYTES = 16 * 2**20
UPDATES = 5
RUN = 6
FINISHED = 4
TURNS = 6


def mixture(fraction):
    gamma_sum = GAMMA_GAS + GAMMA_SLOPE * fraction
    stiff_sum = STIFF_SLOPE * fraction
    if STIFF_GAS != 0.0:
        stiff_sum = stiff_sum + STIFF_GAS
    return gamma_sum, stiff_sum


def initial_cells(labels, jitter):
    def lookup(table):
        return jnp.where(labels == 0, table[0], jnp.where(labels == 1, table[1], table[2]))

    fraction = lookup(ALPHA_TABLE)
    part_one = fraction * lookup(LIQUID_TABLE) * jitter
    part_two = (1.0 - fraction) * lookup(GAS_TABLE) * jitter
    speed = lookup(VELOCITY_TABLE)
    pressure = lookup(PRESSURE_TABLE) * jitter
    return part_one, part_two, speed, pressure, fraction


def ambient_cell():
    fraction = ALPHA_TABLE[0]
    part_one = fraction * LIQUID_TABLE[0]
    part_two = (1.0 - fraction) * GAS_TABLE[0]
    density = part_one + part_two
    speed, pressure = VELOCITY_TABLE[0], PRESSURE_TABLE[0]
    gamma_sum, stiff_sum = mixture(fraction)
    energy = gamma_sum * pressure + stiff_sum + 0.5 * density * speed * speed
    return part_one, part_two, density * speed, 0.0, energy, fraction


def celerity_of(density, pressure, gamma_sum, stiff_sum):
    top = gamma_sum * pressure + stiff_sum + pressure
    return top * lax.rsqrt(top * (gamma_sum * density))


def weno_terms(ha, hb, da, db, dc, ta, tb, tc, ga, gb):
    smooth_zero = ta + ha * (ha + da)
    smooth_one = tb + ha * hb
    smooth_two = tc + hb * (hb - dc)
    square_zero = smooth_zero * smooth_zero
    square_one = smooth_one * smooth_one
    square_two = smooth_two * smooth_two
    weight_zero = square_one * square_two
    weight_one = square_zero * square_two
    weight_two = square_zero * square_one
    low = weight_zero * ga
    high = weight_two * gb
    common = 6.0 * weight_one + (weight_zero + weight_two)
    upper = (low + 1.5 * high) / (common + (weight_two + weight_two))
    lower = (high + 1.5 * low) / (common + (weight_zero + weight_zero))
    return upper, lower


def weno_cell(cells):
    m2, m1, c, p1, p2 = cells
    h0, ha, hb, h3 = (0.5 * (y - x) for x, y in ((m2, m1), (m1, c), (c, p1), (p1, p2)))
    da, db, dc = ha - h0, hb - ha, h3 - hb
    ta, tb, tc = (d * (d * (4.0 / 3.0)) + 0.25 * WENO_EPS for d in (da, db, dc))
    qa, qb, qc = (d * (2.0 / 3.0) for d in (da, db, dc))
    upper, lower = weno_terms(ha, hb, da, db, dc, ta, tb, tc, qb - qa, qc - qb)
    base = c + qb
    return base + ha - upper, base - hb + lower


def weno_run(w, count):
    h = 0.5 * (w[1:] - w[:-1])
    d = h[1:] - h[:-1]
    t = d * (d * (4.0 / 3.0)) + 0.25 * WENO_EPS
    q = d * (2.0 / 3.0)
    g = q[1:] - q[:-1]
    n = count
    ha, hb = h[1 : n + 1], h[2 : n + 2]
    upper, lower = weno_terms(
        ha, hb, d[:n], d[1 : n + 1], d[2:], t[:n], t[1 : n + 1], t[2:], g[:n], g[1:]
    )
    base = w[2 : n + 2] + q[1 : n + 1]
    return base + ha - upper, base - hb + lower


def hllc(left, right, normal):
    tangent = 5 - normal

    def side(state):
        density = state[0] + state[1]
        gamma_sum, stiff_sum = mixture(state[5])
        inner = gamma_sum * state[4] + stiff_sum
        top = inner + state[4]
        return density, inner, top * lax.rsqrt(top * (gamma_sum * density))

    rho_l, inner_l, c_l = side(left)
    rho_r, inner_r, c_r = side(right)
    n_l, n_r, p_l, p_r = left[normal], right[normal], left[4], right[4]
    low = jnp.minimum(n_l - c_l, n_r - c_r)
    high = jnp.maximum(n_l + c_l, n_r + c_r)
    mass_l = rho_l * (low - n_l)
    mass_r = rho_r * (high - n_r)
    star = (p_r - p_l + mass_l * n_l - mass_r * n_r) / (mass_l - mass_r)
    forward = star >= 0.0
    outer_left = low >= 0.0
    pick = jnp.logical_or(outer_left, forward)

    def chosen(a, b):
        return jnp.where(pick, a, b)

    q_one, q_two = chosen(left[0], right[0]), chosen(left[1], right[1])
    n, t, p = chosen(n_l, n_r), chosen(left[tangent], right[tangent]), chosen(p_l, p_r)
    wave, mass, inner = chosen(low, high), chosen(mass_l, mass_r), chosen(inner_l, inner_r)
    rho = q_one + q_two
    energy = inner + 0.5 * rho * (n * n + t * t)
    plain = jnp.logical_or(outer_left, jnp.logical_and(jnp.logical_not(pick), high < 0.0))
    inverse = 1.0 / (wave - star)
    factor = (wave - n) * inverse
    jump = star - n
    star_energy = factor * energy + jump * (rho * factor * star + p * inverse)
    star_pressure = p + mass * jump
    speed = jnp.where(plain, n, star)
    scaled = jnp.where(plain, n, factor * star)
    energy = jnp.where(plain, energy, star_energy)
    p = jnp.where(plain, p, star_pressure)
    carried = rho * scaled
    along = carried * speed + p
    across = carried * t
    moments = (along, across) if normal == 2 else (across, along)
    fraction = star * jnp.where(forward, left[5], right[5])
    return [q_one * scaled, q_two * scaled, *moments, (energy + p) * speed, fraction, star]


def far_first(size):
    return sorted(range(size), key=lambda d: -min(d, size - d))


def kernel(
    sizes,
    labels_hbm,
    jitter_hbm,
    fields,
    steps_ref,
    own_labels,
    own_jitter,
    labels,
    jitter,
    axial_cells,
    radial_cells,
    base,
    upper,
    lower,
    axial_rate,
    radial_rate,
    turned,
    total,
    strip,
    strip_rate,
    dt_ref,
    send_axial,
    send_radial,
    recv_axial,
    recv_radial,
    max_first,
    max_second,
    got_first,
    got_second,
    local_sem,
    shift_send,
    shift_recv,
    halo_send,
    halo_recv,
    first_send,
    first_recv,
    second_send,
    second_recv,
):
    z_size, x_size, core_size, rad_size = sizes
    ax_size = z_size * x_size * core_size
    ax, rad = lax.axis_index("ax"), lax.axis_index("rad")
    core = lax.rem(ax, core_size)
    x = lax.rem(lax.div(ax, core_size), x_size)
    z = lax.div(ax, core_size * x_size)

    def at(z, x, core, rad):
        return ((z * x_size + x) * core_size + core, rad)

    first_group = [
        at(lax.rem(z + dz, z_size), x, lax.rem(core + dc, core_size), rad)
        for dz in far_first(z_size)
        for dc in range(core_size)
        if (dz, dc) != (0, 0)
    ]
    second_group = [
        at(z, lax.rem(x + dx, x_size), core, lax.rem(rad + dr, rad_size))
        for dx in far_first(x_size)
        for dr in far_first(rad_size)
        if (dx, dr) != (0, 0)
    ]
    ax_next = (lax.rem(ax + 1, ax_size), rad)
    ax_last = (lax.rem(ax + ax_size - 1, ax_size), rad)
    rad_next = (ax, lax.rem(rad + 1, rad_size))
    rad_last = (ax, lax.rem(rad + rad_size - 1, rad_size))

    block_first = ax == ax_size - 1
    block_last = ax == ax_size - 2
    wall = rad == 0
    outer = rad == rad_size - 1

    lane = lax.broadcasted_iota(jnp.int32, (ROWS, LANES), 1)
    row = lax.broadcasted_iota(jnp.int32, (ROWS, LANES), 0)

    copies = [
        pltpu.make_async_copy(labels_hbm, own_labels, local_sem.at[0]),
        pltpu.make_async_copy(jitter_hbm, own_jitter, local_sem.at[1]),
    ]
    for copy in copies:
        copy.start()
    barrier = pltpu.get_barrier_semaphore()
    greeted = first_group + second_group + [ax_next, ax_last]
    for device in greeted:
        pl.semaphore_signal(barrier, inc=1, device_id=device, device_id_type=MESH)
    for copy in copies:
        copy.wait()

    def first_copies(step):
        return [
            pltpu.make_async_remote_copy(
                src_ref=max_first.at[step],
                dst_ref=got_first.at[step, i],
                send_sem=first_send.at[step],
                recv_sem=first_recv.at[step],
                device_id=device,
                device_id_type=MESH,
            )
            for i, device in enumerate(first_group)
        ]

    def second_copies(step):
        return [
            pltpu.make_async_remote_copy(
                src_ref=max_second.at[step],
                dst_ref=got_second.at[step, i],
                send_sem=second_send.at[step],
                recv_sem=second_recv.at[step],
                device_id=device,
                device_id_type=MESH,
            )
            for i, device in enumerate(second_group)
        ]

    def whole_phase(step, second):
        got, send, recv, group = (
            (got_second, second_send, second_recv, second_group) if second else (got_first, first_send, first_recv, first_group)
        )
        return pltpu.make_async_remote_copy(
            src_ref=got.at[step],
            dst_ref=got.at[step],
            send_sem=send.at[step],
            recv_sem=recv.at[step],
            device_id=group[0],
            device_id_type=MESH,
        )

    def halo_copies(stage, which=(0, 1, 2, 3)):
        parity = lax.rem(stage, 2)
        pairs = [
            (send_axial.at[1], recv_axial.at[stage, 0], ax_next),
            (send_axial.at[0], recv_axial.at[stage, 1], ax_last),
            (send_radial.at[1], recv_radial.at[stage, 0], rad_next),
            (send_radial.at[0], recv_radial.at[stage, 1], rad_last),
        ]
        return [
            pltpu.make_async_remote_copy(
                src_ref=source,
                dst_ref=target,
                send_sem=halo_send.at[parity, i],
                recv_sem=halo_recv.at[parity, i],
                device_id=device,
                device_id_type=MESH,
            )
            for i, (source, target, device) in enumerate(pairs)
            if i in which
        ]

    def own_speed(t, most):
        part_one, part_two, speed, pressure, fraction = initial_cells(
            own_labels[pl.ds(t * ROWS, ROWS), :], own_jitter[pl.ds(t * ROWS, ROWS), :]
        )
        celerity = celerity_of(part_one + part_two, pressure, *mixture(fraction))
        return jnp.maximum(most, jnp.abs(speed) + celerity)

    most = lax.fori_loop(0, TILES, own_speed, jnp.zeros((ROWS, LANES), jnp.float32))
    max_first[0] = jnp.max(most, axis=0, keepdims=True)

    pl.semaphore_wait(barrier, len(greeted))
    for copy in first_copies(0):
        copy.start()
    shifts = [
        pltpu.make_async_remote_copy(
            src_ref=source,
            dst_ref=target,
            send_sem=shift_send.at[i],
            recv_sem=shift_recv.at[i],
            device_id=ax_last,
            device_id_type=MESH,
        )
        for i, (source, target) in enumerate(((labels_hbm, labels), (jitter_hbm, jitter)))
    ]
    for copy in shifts:
        copy.start()
    for copy in shifts:
        copy.wait()

    def second_phase(step):
        whole_phase(step, False).wait_recv()
        max_second[step] = jnp.maximum(max_first[step], jnp.max(got_first[step], axis=0))
        for copy in second_copies(step):
            copy.start()

    second_phase(0)

    to_lanes = (lane % ROWS) * TILES + lane // ROWS
    def start_cells(t, carry):
        rows = pl.ds(t, ROWS, stride=TILES)
        part_one, part_two, speed, pressure, fraction = initial_cells(
            jnp.take_along_axis(labels[rows, :], to_lanes, axis=1), jnp.take_along_axis(jitter[rows, :], to_lanes, axis=1)
        )
        density = part_one + part_two
        gamma_sum, stiff_sum = mixture(fraction)
        still = jnp.zeros_like(density)
        energy = gamma_sum * pressure + stiff_sum + 0.5 * density * speed * speed
        for i, value in enumerate((part_one, part_two, density * speed, still, energy, fraction)):
            fields[i, t] = value
            base[i, t] = value
        for i, value in enumerate((part_one, part_two, speed, still, pressure, fraction)):
            axial_cells[i, GHOST + t] = value
        return carry

    lax.fori_loop(0, TILES, start_cells, 0)

    radius = (rad * LANES + to_lanes).astype(jnp.float32) + 0.5
    per_radius = 1.0 / radius

    def take_rims(cells, send):
        for i in range(6):
            for k in range(GHOST):
                send[0, 3 * i + k] = cells[i, GHOST + k, 0:1, :]
                send[1, 3 * i + k] = cells[i, TILES + k, ROWS - 1 : ROWS, :]

    def wrapped(cells):
        for i in range(6):
            for k in range(GHOST):
                cells[i, k] = pltpu.roll(cells[i, TILES + k], 1, 0)
                cells[i, GHOST + TILES + k] = pltpu.roll(cells[i, GHOST + k], ROWS - 1, 0)

    def own_strip(cells, which):
        for i in range(6):
            q = {2: 3, 3: 2}.get(i, i) if which else i
            for k in range(6):
                strip[q, which, 2 * k + 6 : 2 * k + 7, :] = cells[i, GHOST + k, 0:1, :]
                strip[q, which, 2 * k + 1 : 2 * k + 2, :] = cells[i, GHOST + 10 + k, ROWS - 1 : ROWS, :]

    def rim_strip(recv, stage, which, at_low, at_high):
        for i in range(6):
            q = {2: 3, 3: 2}.get(i, i) if which else i
            high = strip[q, which, 11:12, :]
            for k in range(GHOST):
                if which:
                    low = strip[q, which, 10 - 2 * k : 11 - 2 * k, :]
                    if i == 3:
                        low = -low
                else:
                    low = strip[q, which, 6:7, :]
                strip[q, which, 2 * k : 2 * k + 1, :] = jnp.where(at_low, low, recv[stage, 0, 3 * i + k])
                strip[q, which, 2 * k + 13 : 2 * k + 14, :] = jnp.where(at_high, high, recv[stage, 1, 3 * i + k])

    def strip_rates():
        left, right = [], []
        for i in range(6):
            w = [strip[i, :, 2 * k : 2 * k + 8, :] for k in range(6)]
            left.append(weno_cell(w[:5])[0])
            right.append(weno_cell(w[1:])[1])
            if i == 5:
                fraction = w[3]
        flux = hllc(left, right, 2)
        change = [value - pltpu.roll(value, ROWS - 2, 1) for value in flux]
        change[5] = change[5] - fraction * change[6]
        for i in range(6):
            strip_rate[i] = change[i]
        for i in range(6):
            q = {2: 3, 3: 2}.get(i, i)
            for k in range(GHOST):
                axial_rate[i, 1 + k, 0:1, :] = strip_rate[i, 0, 2 * k : 2 * k + 1, :]
                axial_rate[i, TILES - 2 + k, ROWS - 1 : ROWS, :] = strip_rate[i, 0, 2 * k + 1 : 2 * k + 2, :]
                radial_rate[i, 1 + k, 0:1, :] = strip_rate[q, 1, 2 * k : 2 * k + 1, :]
                radial_rate[i, TILES - 2 + k, ROWS - 1 : ROWS, :] = strip_rate[q, 1, 2 * k + 1 : 2 * k + 2, :]

    def rim_ghosts(cells, recv, stage, which, at_low, at_high):
        for i in range(6):
            high = cells[i, GHOST + TILES - 1, ROWS - 1 : ROWS, :]
            for k in range(GHOST):
                if which:
                    low = cells[i, 2 * GHOST - 1 - k, 0:1, :]
                    if i == 3:
                        low = -low
                else:
                    low = cells[i, GHOST, 0:1, :]
                cells[i, k, 0:1, :] = jnp.where(at_low, low, recv[stage, 0, 3 * i + k])
                cells[i, GHOST + TILES + k, ROWS - 1 : ROWS, :] = jnp.where(at_high, high, recv[stage, 1, 3 * i + k])

    def states(cells, which, runs):
        def one(i, carry):
            for first, count in runs:
                up, down = weno_run(cells[i, first : first + count + 4], count)
                upper[which, i, first : first + count] = up
                lower[which, i, first : first + count] = down
            return carry

        lax.fori_loop(0, 6, one, 0)

    def face(which, f, normal):
        return hllc([upper[which, i, f] for i in range(6)], [lower[which, i, f + 1] for i in range(6)], normal)

    def faces(cells, which, rate, normal, first, below, rounds, count, stride):
        def some(r, below):
            for k in range(count):
                f = first + r * stride + k
                above = face(which, f, normal)
                change = [b - a for b, a in zip(below, above)]
                change[5] = change[5] - cells[5, f + 2] * change[6]
                for i in range(6):
                    rate[i, f] = change[i]
                below = tuple(above)
            return below

        lax.fori_loop(0, rounds, some, below)

    still = (jnp.zeros((ROWS, LANES), jnp.float32),) * 7

    def radial_sweep():
        states(radial_cells, 1, [(first, RUN) for first in range(0, TILES + 2, RUN)])
        faces(radial_cells, 1, radial_rate, 3, 0, still, (TILES + 2) // FACES, FACES, FACES)

    def axial_ends():
        states(axial_cells, 0, [(0, 6), (12, 6)])
        faces(axial_cells, 0, axial_rate, 2, 0, still, 2, 4, 13)

    def axial_middle():
        states(axial_cells, 0, [(6, 6)])
        faces(axial_cells, 0, axial_rate, 2, 4, tuple(face(0, 3, 2)), 2, 5, 5)

    def send_axial_rims(stage, cells=axial_cells):
        take_rims(cells, send_axial)
        for copy in halo_copies(stage, (0, 1)):
            copy.start()

    def turn_cells(axial, radial):
        def turn(r, carry):
            for k in range(TURNS):
                i = r * TURNS + k
                block = axial[i, GHOST : GHOST + TILES].reshape(LANES, LANES)
                radial[i, GHOST : GHOST + TILES] = block.T.reshape(TILES, ROWS, LANES)
            return carry

        lax.fori_loop(0, 6 // TURNS, turn, 0)

    def send_radial_rims(stage, cells=radial_cells):
        take_rims(cells, send_radial)
        for copy in halo_copies(stage, (2, 3)):
            copy.start()

    def whole_rate(t, q_one, q_two, u, v, p, a, energy):
        over = v * per_radius
        carried = (q_one + q_two) * over
        source = (q_one * over, q_two * over, u * carried, v * carried, (energy + p) * over)
        change = [axial_rate[i, t + 1] + turned[i, t] for i in range(6)]
        return [change[i] - source[i] for i in range(5)] + [change[5]]

    def primitives(fields):
        density = fields[0] + fields[1]
        gamma_sum, stiff_sum = mixture(fields[5])
        inverse = 1.0 / (density * gamma_sum)
        per_density = inverse * gamma_sum
        u = fields[2] * per_density
        v = fields[3] * per_density
        p = (fields[4] - 0.5 * (fields[2] * u + fields[3] * v) - stiff_sum) * (inverse * density)
        return fields[0], fields[1], u, v, p, fields[5]

    def advance_rims(recv, stage):
        dt = dt_ref[0:1, :]
        for side in range(2):
            old = [recv[stage - 1, side, 3 * i : 3 * i + 3] for i in range(6)]
            change = [recv[stage, side, 3 * i : 3 * i + 3] for i in range(6)]
            q_one, q_two, u, v, p, a = old
            density = q_one + q_two
            gamma_sum, stiff_sum = mixture(a)
            energy = gamma_sum * p + stiff_sum + 0.5 * density * (u * u + v * v)
            before = (q_one, q_two, density * u, density * v, energy, a)
            for i, value in enumerate(primitives([b + dt * c for b, c in zip(before, change)])):
                recv[stage, side, 3 * i : 3 * i + 3] = value

    dt_ref[...] = jnp.zeros_like(dt_ref)
    send_axial_rims(0)
    turn_cells(axial_cells, radial_cells)
    send_radial_rims(0)

    def stage_body(stage, carry):
        step = lax.div(stage, 3)
        section = stage - 3 * step
        halos = halo_copies(stage)

        wrapped(axial_cells)
        wrapped(radial_cells)

        early = jnp.logical_and(section == 1, step > 0)

        @pl.when(early)
        def _():
            for copy in halos:
                copy.wait_recv()
            advance_rims(recv_axial, stage)
            advance_rims(recv_radial, stage)
            rim_ghosts(axial_cells, recv_axial, stage, 0, block_first, block_last)
            rim_ghosts(radial_cells, recv_radial, stage, 1, wall, outer)

        radial_sweep()
        axial_ends()

        @pl.when(jnp.logical_not(early))
        def _():
            axial_middle()
            steps_ref[step] = jnp.max(dt_ref[...])
            own_strip(axial_cells, 0)
            own_strip(radial_cells, 1)
            for copy in halo_copies(stage):
                copy.wait_recv()

            @pl.when(section == 1)
            def _():
                advance_rims(recv_axial, stage)
                advance_rims(recv_radial, stage)

            rim_strip(recv_axial, stage, 0, block_first, block_last)
            rim_strip(recv_radial, stage, 1, wall, outer)
            strip_rates()

        @pl.when(jnp.logical_and(section == 0, step > 0))
        def _():
            second_phase(step)

        def turn_back(r, carry):
            for k in range(TURNS):
                i = r * TURNS + k
                block = radial_rate[i, 1 : 1 + TILES].reshape(LANES, LANES)
                turned[i] = block.T.reshape(TILES, ROWS, LANES)
            return carry

        lax.fori_loop(0, 6 // TURNS, turn_back, 0)

        for copy in halos:
            copy.wait_send()

        @pl.when(section == 0)
        def _():
            def rates(t, carry):
                for i, value in enumerate(whole_rate(t, *(axial_cells[i, GHOST + t] for i in range(6)), fields[4, t])):
                    total[0, i, GHOST + t] = value
                return carry

            lax.fori_loop(0, TILES, rates, 0)
            send_axial_rims(stage + 1, total.at[0])
            turn_cells(total.at[0], total.at[1])
            send_radial_rims(stage + 1, total.at[1])
            whole_phase(step, True).wait_recv()
            top = jnp.maximum(max_second[step], jnp.max(got_second[step], axis=0))
            dt = CFL_NUMBER / jnp.broadcast_to(jnp.max(top, axis=1, keepdims=True), (ROWS, LANES))
            dt_ref[...] = dt
            whole_phase(step, True).wait_send()
            whole_phase(step, False).wait_send()

        third = jnp.float32(1.0 / 3.0)
        keep = jnp.where(section == 0, 0.0, jnp.where(section == 1, 0.75, third))
        take = jnp.where(section == 0, 1.0, jnp.where(section == 1, 0.25, jnp.float32(2.0 / 3.0)))
        closing = section == 2
        dt = dt_ref[...]

        def update(tiles, most):
            for t in tiles:
                old = [fields[i, t] for i in range(6)]
                change = whole_rate(t, *(axial_cells[i, GHOST + t] for i in range(6)), old[4])
                new = []
                for i in range(6):
                    start = base[i, t]
                    value = keep * start + take * (old[i] + dt * change[i])
                    fields[i, t] = value
                    base[i, t] = jnp.where(closing, value, start)
                    new.append(value)
                q_one, q_two, u, v, p, a = primitives(new)
                for i, value in enumerate((q_one, q_two, u, v, p, a)):
                    axial_cells[i, GHOST + t] = value
                density = q_one + q_two
                gamma_sum, stiff_sum = mixture(a)
                speed = jnp.abs(u) + jnp.abs(v) + celerity_of(density, p, gamma_sum, stiff_sum)
                most = jnp.maximum(most, speed)
            return most

        most = lax.fori_loop(
            0,
            GHOST // RIMS,
            lambda r, m: update([base_tile + r * RIMS + k for k in range(RIMS) for base_tile in (0, TILES - GHOST)], m),
            jnp.zeros((ROWS, LANES), jnp.float32),
        )

        @pl.when(jnp.logical_and(section > 0, stage < STAGES - 1))
        def _():
            send_axial_rims(stage + 1)

        @pl.when(early)
        def _():
            axial_middle()

        most = lax.fori_loop(
            0,
            (TILES - 2 * GHOST) // UPDATES,
            lambda r, m: update([GHOST + r * UPDATES + k for k in range(UPDATES)], m),
            most,
        )

        @pl.when(jnp.logical_and(closing, step < STEPS - 1))
        def _():
            max_first[step + 1] = jnp.max(most, axis=0, keepdims=True)
            for copy in first_copies(step + 1):
                copy.start()

        @pl.when(stage < STAGES - 1)
        def _():
            turn_cells(axial_cells, radial_cells)

        @pl.when(jnp.logical_and(section > 0, stage < STAGES - 1))
        def _():
            send_radial_rims(stage + 1)

        return carry

    lax.fori_loop(0, STAGES, stage_body, 0)


def finish(ax_size, fields, steps, out_ref, steps_ref):
    outside = lax.axis_index("ax") == ax_size - 1
    lane = lax.broadcasted_iota(jnp.int32, (ROWS, LANES), 1)
    from_lanes = (lane % TILES) * ROWS + lane // TILES
    for i in range(STEPS):
        steps_ref[i] = steps[i]

    def one(r, carry):
        for k in range(FINISHED):
            t = r * FINISHED + k
            for i, value in enumerate(ambient_cell()):
                moved = jnp.take_along_axis(fields[i, t], from_lanes, axis=1)
                out_ref[i, pl.ds(t, ROWS, stride=TILES), :] = jnp.where(outside, jnp.float32(value), moved)
        return carry

    lax.fori_loop(0, TILES // FINISHED, one, 0)


def solution(mesh):
    ax_size, rad_size = mesh.shape["ax"], mesh.shape["rad"]
    sizes = (ax_size // (2 * X_CHIPS), X_CHIPS, 2, rad_size)
    first = sizes[0] * sizes[2] - 1
    second = sizes[1] * sizes[3] - 1

    def shards(labels, jitter):
        block = labels.shape
        f32 = jnp.float32
        tile = (TILES, ROWS, LANES)
        dma = pltpu.SemaphoreType.DMA
        labels, jitter = (pltpu.with_memory_space_constraint(a, pltpu.HBM) for a in (labels, jitter))
        fields, steps = pl.pallas_call(
            functools.partial(kernel, sizes),
            out_shape=(jax.ShapeDtypeStruct((6, *tile), f32), jax.ShapeDtypeStruct((STEPS,), f32)),
            in_specs=[pl.BlockSpec(memory_space=pltpu.HBM)] * 2,
            out_specs=(pl.BlockSpec(memory_space=pltpu.VMEM), pl.BlockSpec(memory_space=pltpu.SMEM)),
            scratch_shapes=[
                pltpu.VMEM(block, jnp.int32),
                pltpu.VMEM(block, f32),
                pltpu.VMEM(block, jnp.int32),
                pltpu.VMEM(block, f32),
                pltpu.VMEM((6, TILES + 2 * GHOST, ROWS, LANES), f32),
                pltpu.VMEM((6, TILES + 2 * GHOST, ROWS, LANES), f32),
                pltpu.VMEM((6, *tile), f32),
                pltpu.VMEM((2, 6, TILES + 3, ROWS, LANES), f32),
                pltpu.VMEM((2, 6, TILES + 3, ROWS, LANES), f32),
                pltpu.VMEM((6, TILES + 2, ROWS, LANES), f32),
                pltpu.VMEM((6, TILES + 2, ROWS, LANES), f32),
                pltpu.VMEM((6, *tile), f32),
                pltpu.VMEM((2, 6, TILES + 2 * GHOST, ROWS, LANES), f32),
                pltpu.VMEM((6, 2, 24, LANES), f32),
                pltpu.VMEM((6, 2, ROWS, LANES), f32),
                pltpu.VMEM((ROWS, LANES), f32),
                pltpu.VMEM((2, 18, 1, LANES), f32),
                pltpu.VMEM((2, 18, 1, LANES), f32),
                pltpu.VMEM((STAGES, 2, 18, 1, LANES), f32),
                pltpu.VMEM((STAGES, 2, 18, 1, LANES), f32),
                pltpu.VMEM((STEPS, 1, LANES), f32),
                pltpu.VMEM((STEPS, 1, LANES), f32),
                pltpu.VMEM((STEPS, first, 1, LANES), f32),
                pltpu.VMEM((STEPS, second, 1, LANES), f32),
                dma((2,)),
                dma((2,)),
                dma((2,)),
                dma((2, 4)),
                dma((2, 4)),
                dma((STEPS,)),
                dma((STEPS,)),
                dma((STEPS,)),
                dma((STEPS,)),
            ],
            compiler_params=pltpu.CompilerParams(
                collective_id=0, has_side_effects=True, vmem_limit_bytes=VMEM_BYTES
            ),
        )(labels, jitter)
        return pl.pallas_call(
            functools.partial(finish, ax_size),
            out_shape=(jax.ShapeDtypeStruct((6, *block), f32), jax.ShapeDtypeStruct((STEPS,), f32)),
            in_specs=[pl.BlockSpec(memory_space=pltpu.VMEM), pl.BlockSpec(memory_space=pltpu.SMEM)],
            out_specs=(pl.BlockSpec(memory_space=pltpu.VMEM), pl.BlockSpec(memory_space=pltpu.SMEM)),
            compiler_params=pltpu.CompilerParams(vmem_limit_bytes=VMEM_BYTES),
        )(fields, steps)

    return jax.shard_map(
        shards, mesh=mesh, in_specs=(P("ax", "rad"),) * 2, out_specs=(P(None, "ax", "rad"), P()), check_vma=False
    )
```

```python
import functools

import jax
import jax.numpy as jnp
from jax import lax
from jax.experimental import pallas as pl
from jax.experimental.pallas import tpu as pltpu
from jax.sharding import PartitionSpec as P

MESH = pl.DeviceIdType.MESH

STEPS = 3
STAGES = 3 * STEPS
X_CHIPS = 4

G_LIQUID = 4.4
PI_LIQUID = 1.0
G_GAS = 1.4
PI_GAS = 0.0
CFL_NUMBER = 0.3
WENO_EPS = 1e-06
ALPHA_TABLE = (0.99, 0.99, 0.01)
LIQUID_TABLE = (1.0, 1.25, 1.0)
GAS_TABLE = (0.1, 0.1, 0.1)
VELOCITY_TABLE = (0.0, 0.4, 0.0)
PRESSURE_TABLE = (1.0, 3.0, 1.0)

GAMMA_GAS = 1.0 / (G_GAS - 1.0)
GAMMA_SLOPE = 1.0 / (G_LIQUID - 1.0) - GAMMA_GAS
STIFF_GAS = G_GAS * PI_GAS / (G_GAS - 1.0)
STIFF_SLOPE = G_LIQUID * PI_LIQUID / (G_LIQUID - 1.0) - STIFF_GAS

TILES = 16
ROWS = 8
LANES = 128
GHOST = 3
FACES = 3
RIMS = 3
VMEM_BYTES = 16 * 2**20
UPDATES = 5
RUN = 6
FINISHED = 4
TURNS = 6


def mixture(fraction):
    gamma_sum = GAMMA_GAS + GAMMA_SLOPE * fraction
    stiff_sum = STIFF_SLOPE * fraction
    if STIFF_GAS != 0.0:
        stiff_sum = stiff_sum + STIFF_GAS
    return gamma_sum, stiff_sum


def initial_cells(labels, jitter):
    def lookup(table):
        return jnp.where(labels == 0, table[0], jnp.where(labels == 1, table[1], table[2]))

    fraction = lookup(ALPHA_TABLE)
    part_one = fraction * lookup(LIQUID_TABLE) * jitter
    part_two = (1.0 - fraction) * lookup(GAS_TABLE) * jitter
    speed = lookup(VELOCITY_TABLE)
    pressure = lookup(PRESSURE_TABLE) * jitter
    return part_one, part_two, speed, pressure, fraction


def ambient_cell():
    fraction = ALPHA_TABLE[0]
    part_one = fraction * LIQUID_TABLE[0]
    part_two = (1.0 - fraction) * GAS_TABLE[0]
    density = part_one + part_two
    speed, pressure = VELOCITY_TABLE[0], PRESSURE_TABLE[0]
    gamma_sum, stiff_sum = mixture(fraction)
    energy = gamma_sum * pressure + stiff_sum + 0.5 * density * speed * speed
    return part_one, part_two, density * speed, 0.0, energy, fraction


def celerity_of(density, pressure, gamma_sum, stiff_sum):
    top = gamma_sum * pressure + stiff_sum + pressure
    return top * lax.rsqrt(top * (gamma_sum * density))


def weno_terms(ha, hb, da, db, dc, ta, tb, tc, ga, gb):
    smooth_zero = ta + ha * (ha + da)
    smooth_one = tb + ha * hb
    smooth_two = tc + hb * (hb - dc)
    square_zero = smooth_zero * smooth_zero
    square_one = smooth_one * smooth_one
    square_two = smooth_two * smooth_two
    weight_zero = square_one * square_two
    weight_one = square_zero * square_two
    weight_two = square_zero * square_one
    low = weight_zero * ga
    high = weight_two * gb
    common = 6.0 * weight_one + (weight_zero + weight_two)
    upper = (low + 1.5 * high) / (common + (weight_two + weight_two))
    lower = (high + 1.5 * low) / (common + (weight_zero + weight_zero))
    return upper, lower


def weno_cell(cells):
    m2, m1, c, p1, p2 = cells
    h0, ha, hb, h3 = (0.5 * (y - x) for x, y in ((m2, m1), (m1, c), (c, p1), (p1, p2)))
    da, db, dc = ha - h0, hb - ha, h3 - hb
    ta, tb, tc = (d * (d * (4.0 / 3.0)) + 0.25 * WENO_EPS for d in (da, db, dc))
    qa, qb, qc = (d * (2.0 / 3.0) for d in (da, db, dc))
    upper, lower = weno_terms(ha, hb, da, db, dc, ta, tb, tc, qb - qa, qc - qb)
    base = c + qb
    return base + ha - upper, base - hb + lower


def weno_run(w, count):
    h = 0.5 * (w[1:] - w[:-1])
    d = h[1:] - h[:-1]
    t = d * (d * (4.0 / 3.0)) + 0.25 * WENO_EPS
    q = d * (2.0 / 3.0)
    g = q[1:] - q[:-1]
    n = count
    ha, hb = h[1 : n + 1], h[2 : n + 2]
    upper, lower = weno_terms(
        ha, hb, d[:n], d[1 : n + 1], d[2:], t[:n], t[1 : n + 1], t[2:], g[:n], g[1:]
    )
    base = w[2 : n + 2] + q[1 : n + 1]
    return base + ha - upper, base - hb + lower


def hllc(left, right, normal):
    tangent = 5 - normal

    def side(state):
        density = state[0] + state[1]
        gamma_sum, stiff_sum = mixture(state[5])
        inner = gamma_sum * state[4] + stiff_sum
        top = inner + state[4]
        return density, inner, top * lax.rsqrt(top * (gamma_sum * density))

    rho_l, inner_l, c_l = side(left)
    rho_r, inner_r, c_r = side(right)
    n_l, n_r, p_l, p_r = left[normal], right[normal], left[4], right[4]
    low = jnp.minimum(n_l - c_l, n_r - c_r)
    high = jnp.maximum(n_l + c_l, n_r + c_r)
    mass_l = rho_l * (low - n_l)
    mass_r = rho_r * (high - n_r)
    star = (p_r - p_l + mass_l * n_l - mass_r * n_r) / (mass_l - mass_r)
    forward = star >= 0.0
    outer_left = low >= 0.0
    pick = jnp.logical_or(outer_left, forward)

    def chosen(a, b):
        return jnp.where(pick, a, b)

    q_one, q_two = chosen(left[0], right[0]), chosen(left[1], right[1])
    n, t, p = chosen(n_l, n_r), chosen(left[tangent], right[tangent]), chosen(p_l, p_r)
    wave, mass, inner = chosen(low, high), chosen(mass_l, mass_r), chosen(inner_l, inner_r)
    rho = q_one + q_two
    energy = inner + 0.5 * rho * (n * n + t * t)
    plain = jnp.logical_or(outer_left, jnp.logical_and(jnp.logical_not(pick), high < 0.0))
    inverse = 1.0 / (wave - star)
    factor = (wave - n) * inverse
    jump = star - n
    star_energy = factor * energy + jump * (rho * factor * star + p * inverse)
    star_pressure = p + mass * jump
    speed = jnp.where(plain, n, star)
    scaled = jnp.where(plain, n, factor * star)
    energy = jnp.where(plain, energy, star_energy)
    p = jnp.where(plain, p, star_pressure)
    carried = rho * scaled
    along = carried * speed + p
    across = carried * t
    moments = (along, across) if normal == 2 else (across, along)
    fraction = star * jnp.where(forward, left[5], right[5])
    return [q_one * scaled, q_two * scaled, *moments, (energy + p) * speed, fraction, star]


def far_first(size):
    return sorted(range(size), key=lambda d: -min(d, size - d))


def kernel(
    sizes,
    labels_hbm,
    jitter_hbm,
    fields,
    steps_ref,
    own_labels,
    own_jitter,
    labels,
    jitter,
    axial_cells,
    radial_cells,
    base,
    upper,
    lower,
    axial_rate,
    radial_rate,
    turned,
    total,
    strip,
    strip_rate,
    dt_ref,
    send_axial,
    send_radial,
    recv_axial,
    recv_radial,
    max_first,
    max_second,
    got_first,
    got_second,
    local_sem,
    shift_send,
    shift_recv,
    halo_send,
    halo_recv,
    first_send,
    first_recv,
    second_send,
    second_recv,
):
    z_size, x_size, core_size, rad_size = sizes
    ax_size = z_size * x_size * core_size
    ax, rad = lax.axis_index("ax"), lax.axis_index("rad")
    core = lax.rem(ax, core_size)
    x = lax.rem(lax.div(ax, core_size), x_size)
    z = lax.div(ax, core_size * x_size)

    def at(z, x, core, rad):
        return ((z * x_size + x) * core_size + core, rad)

    first_group = [
        at(lax.rem(z + dz, z_size), x, lax.rem(core + dc, core_size), rad)
        for dz in far_first(z_size)
        for dc in range(core_size)
        if (dz, dc) != (0, 0)
    ]
    second_group = [
        at(z, lax.rem(x + dx, x_size), core, lax.rem(rad + dr, rad_size))
        for dx in far_first(x_size)
        for dr in far_first(rad_size)
        if (dx, dr) != (0, 0)
    ]
    ax_next = (lax.rem(ax + 1, ax_size), rad)
    ax_last = (lax.rem(ax + ax_size - 1, ax_size), rad)
    rad_next = (ax, lax.rem(rad + 1, rad_size))
    rad_last = (ax, lax.rem(rad + rad_size - 1, rad_size))

    block_first = ax == ax_size - 1
    block_last = ax == ax_size - 2
    wall = rad == 0
    outer = rad == rad_size - 1

    lane = lax.broadcasted_iota(jnp.int32, (ROWS, LANES), 1)
    row = lax.broadcasted_iota(jnp.int32, (ROWS, LANES), 0)

    copies = [
        pltpu.make_async_copy(labels_hbm, own_labels, local_sem.at[0]),
        pltpu.make_async_copy(jitter_hbm, own_jitter, local_sem.at[1]),
    ]
    barrier = pltpu.get_barrier_semaphore()
    greeted = second_group[:8] + first_group[:8] + second_group[8:] + first_group[8:] + [ax_next, ax_last]
    for device in greeted:
        pl.semaphore_signal(barrier, inc=1, device_id=device, device_id_type=MESH)
        if device is greeted[0]:
            for copy in copies:
                copy.start()
    for copy in copies:
        copy.wait()

    def first_copies(step):
        return [
            pltpu.make_async_remote_copy(
                src_ref=max_first.at[step],
                dst_ref=got_first.at[step, i],
                send_sem=first_send.at[step],
                recv_sem=first_recv.at[step],
                device_id=device,
                device_id_type=MESH,
            )
            for i, device in enumerate(first_group)
        ]

    def second_copies(step):
        return [
            pltpu.make_async_remote_copy(
                src_ref=max_second.at[step],
                dst_ref=got_second.at[step, i],
                send_sem=second_send.at[step],
                recv_sem=second_recv.at[step],
                device_id=device,
                device_id_type=MESH,
            )
            for i, device in enumerate(second_group)
        ]

    def whole_phase(step, second):
        got, send, recv, group = (
            (got_second, second_send, second_recv, second_group) if second else (got_first, first_send, first_recv, first_group)
        )
        return pltpu.make_async_remote_copy(
            src_ref=got.at[step],
            dst_ref=got.at[step],
            send_sem=send.at[step],
            recv_sem=recv.at[step],
            device_id=group[0],
            device_id_type=MESH,
        )

    def halo_copies(stage, which=(0, 1, 2, 3)):
        parity = lax.rem(stage, 2)
        pairs = [
            (send_axial.at[1], recv_axial.at[stage, 0], ax_next),
            (send_axial.at[0], recv_axial.at[stage, 1], ax_last),
            (send_radial.at[1], recv_radial.at[stage, 0], rad_next),
            (send_radial.at[0], recv_radial.at[stage, 1], rad_last),
        ]
        return [
            pltpu.make_async_remote_copy(
                src_ref=source,
                dst_ref=target,
                send_sem=halo_send.at[parity, i],
                recv_sem=halo_recv.at[parity, i],
                device_id=device,
                device_id_type=MESH,
            )
            for i, (source, target, device) in enumerate(pairs)
            if i in which
        ]

    def own_speed(t, most):
        part_one, part_two, speed, pressure, fraction = initial_cells(
            own_labels[pl.ds(t * ROWS, ROWS), :], own_jitter[pl.ds(t * ROWS, ROWS), :]
        )
        celerity = celerity_of(part_one + part_two, pressure, *mixture(fraction))
        return jnp.maximum(most, jnp.abs(speed) + celerity)

    most = lax.fori_loop(0, TILES, own_speed, jnp.zeros((ROWS, LANES), jnp.float32))
    max_first[0] = jnp.max(most, axis=0, keepdims=True)

    pl.semaphore_wait(barrier, len(greeted))
    for copy in first_copies(0):
        copy.start()
    shifts = [
        pltpu.make_async_remote_copy(
            src_ref=source,
            dst_ref=target,
            send_sem=shift_send.at[i],
            recv_sem=shift_recv.at[i],
            device_id=ax_last,
            device_id_type=MESH,
        )
        for i, (source, target) in enumerate(((labels_hbm, labels), (jitter_hbm, jitter)))
    ]
    for copy in shifts:
        copy.start()
    for copy in shifts:
        copy.wait()

    def second_phase(step):
        whole_phase(step, False).wait_recv()
        max_second[step] = jnp.maximum(max_first[step], jnp.max(got_first[step], axis=0))
        for copy in second_copies(step):
            copy.start()

    second_phase(0)

    to_lanes = (lane % ROWS) * TILES + lane // ROWS
    def start_cells(t, carry):
        rows = pl.ds(t, ROWS, stride=TILES)
        part_one, part_two, speed, pressure, fraction = initial_cells(
            jnp.take_along_axis(labels[rows, :], to_lanes, axis=1), jnp.take_along_axis(jitter[rows, :], to_lanes, axis=1)
        )
        density = part_one + part_two
        gamma_sum, stiff_sum = mixture(fraction)
        still = jnp.zeros_like(density)
        energy = gamma_sum * pressure + stiff_sum + 0.5 * density * speed * speed
        for i, value in enumerate((part_one, part_two, density * speed, still, energy, fraction)):
            fields[i, t] = value
            base[i, t] = value
        for i, value in enumerate((part_one, part_two, speed, still, pressure, fraction)):
            axial_cells[i, GHOST + t] = value
        return carry

    lax.fori_loop(0, TILES, start_cells, 0)

    radius = (rad * LANES + to_lanes).astype(jnp.float32) + 0.5
    per_radius = 1.0 / radius

    def take_rims(cells, send):
        for i in range(6):
            for k in range(GHOST):
                send[0, 3 * i + k] = cells[i, GHOST + k, 0:1, :]
                send[1, 3 * i + k] = cells[i, TILES + k, ROWS - 1 : ROWS, :]

    def wrapped(cells):
        for i in range(6):
            for k in range(GHOST):
                cells[i, k] = pltpu.roll(cells[i, TILES + k], 1, 0)
                cells[i, GHOST + TILES + k] = pltpu.roll(cells[i, GHOST + k], ROWS - 1, 0)

    def own_strip(cells, which):
        for i in range(6):
            q = {2: 3, 3: 2}.get(i, i) if which else i
            for k in range(6):
                strip[q, which, 2 * k + 6 : 2 * k + 7, :] = cells[i, GHOST + k, 0:1, :]
                strip[q, which, 2 * k + 1 : 2 * k + 2, :] = cells[i, GHOST + 10 + k, ROWS - 1 : ROWS, :]

    def rim_strip(recv, stage, which, at_low, at_high):
        for i in range(6):
            q = {2: 3, 3: 2}.get(i, i) if which else i
            high = strip[q, which, 11:12, :]
            for k in range(GHOST):
                if which:
                    low = strip[q, which, 10 - 2 * k : 11 - 2 * k, :]
                    if i == 3:
                        low = -low
                else:
                    low = strip[q, which, 6:7, :]
                strip[q, which, 2 * k : 2 * k + 1, :] = jnp.where(at_low, low, recv[stage, 0, 3 * i + k])
                strip[q, which, 2 * k + 13 : 2 * k + 14, :] = jnp.where(at_high, high, recv[stage, 1, 3 * i + k])

    def strip_rates():
        left, right = [], []
        for i in range(6):
            w = [strip[i, :, 2 * k : 2 * k + 8, :] for k in range(6)]
            left.append(weno_cell(w[:5])[0])
            right.append(weno_cell(w[1:])[1])
            if i == 5:
                fraction = w[3]
        flux = hllc(left, right, 2)
        change = [value - pltpu.roll(value, ROWS - 2, 1) for value in flux]
        change[5] = change[5] - fraction * change[6]
        for i in range(6):
            strip_rate[i] = change[i]
        for i in range(6):
            q = {2: 3, 3: 2}.get(i, i)
            for k in range(GHOST):
                axial_rate[i, 1 + k, 0:1, :] = strip_rate[i, 0, 2 * k : 2 * k + 1, :]
                axial_rate[i, TILES - 2 + k, ROWS - 1 : ROWS, :] = strip_rate[i, 0, 2 * k + 1 : 2 * k + 2, :]
                radial_rate[i, 1 + k, 0:1, :] = strip_rate[q, 1, 2 * k : 2 * k + 1, :]
                radial_rate[i, TILES - 2 + k, ROWS - 1 : ROWS, :] = strip_rate[q, 1, 2 * k + 1 : 2 * k + 2, :]

    def rim_ghosts(cells, recv, stage, which, at_low, at_high):
        for i in range(6):
            high = cells[i, GHOST + TILES - 1, ROWS - 1 : ROWS, :]
            for k in range(GHOST):
                if which:
                    low = cells[i, 2 * GHOST - 1 - k, 0:1, :]
                    if i == 3:
                        low = -low
                else:
                    low = cells[i, GHOST, 0:1, :]
                cells[i, k, 0:1, :] = jnp.where(at_low, low, recv[stage, 0, 3 * i + k])
                cells[i, GHOST + TILES + k, ROWS - 1 : ROWS, :] = jnp.where(at_high, high, recv[stage, 1, 3 * i + k])

    def states(cells, which, runs):
        def one(i, carry):
            for first, count in runs:
                up, down = weno_run(cells[i, first : first + count + 4], count)
                upper[which, i, first : first + count] = up
                lower[which, i, first : first + count] = down
            return carry

        lax.fori_loop(0, 6, one, 0)

    def face(which, f, normal):
        return hllc([upper[which, i, f] for i in range(6)], [lower[which, i, f + 1] for i in range(6)], normal)

    def faces(cells, which, rate, normal, first, below, rounds, count, stride):
        def some(r, below):
            for k in range(count):
                f = first + r * stride + k
                above = face(which, f, normal)
                change = [b - a for b, a in zip(below, above)]
                change[5] = change[5] - cells[5, f + 2] * change[6]
                for i in range(6):
                    rate[i, f] = change[i]
                below = tuple(above)
            return below

        lax.fori_loop(0, rounds, some, below)

    still = (jnp.zeros((ROWS, LANES), jnp.float32),) * 7

    def radial_sweep():
        states(radial_cells, 1, [(first, RUN) for first in range(0, TILES + 2, RUN)])
        faces(radial_cells, 1, radial_rate, 3, 0, still, (TILES + 2) // FACES, FACES, FACES)

    def axial_ends():
        states(axial_cells, 0, [(0, 6), (12, 6)])
        faces(axial_cells, 0, axial_rate, 2, 0, still, 2, 4, 13)

    def axial_middle():
        states(axial_cells, 0, [(6, 6)])
        faces(axial_cells, 0, axial_rate, 2, 4, tuple(face(0, 3, 2)), 2, 5, 5)

    def send_axial_rims(stage, cells=axial_cells):
        take_rims(cells, send_axial)
        for copy in halo_copies(stage, (0, 1)):
            copy.start()

    def turn_cells(axial, radial):
        def turn(r, carry):
            for k in range(TURNS):
                i = r * TURNS + k
                block = axial[i, GHOST : GHOST + TILES].reshape(LANES, LANES)
                radial[i, GHOST : GHOST + TILES] = block.T.reshape(TILES, ROWS, LANES)
            return carry

        lax.fori_loop(0, 6 // TURNS, turn, 0)

    def send_radial_rims(stage, cells=radial_cells):
        take_rims(cells, send_radial)
        for copy in halo_copies(stage, (2, 3)):
            copy.start()

    def whole_rate(t, q_one, q_two, u, v, p, a, energy):
        over = v * per_radius
        carried = (q_one + q_two) * over
        source = (q_one * over, q_two * over, u * carried, v * carried, (energy + p) * over)
        change = [axial_rate[i, t + 1] + turned[i, t] for i in range(6)]
        return [change[i] - source[i] for i in range(5)] + [change[5]]

    def primitives(fields):
        density = fields[0] + fields[1]
        gamma_sum, stiff_sum = mixture(fields[5])
        inverse = 1.0 / (density * gamma_sum)
        per_density = inverse * gamma_sum
        u = fields[2] * per_density
        v = fields[3] * per_density
        p = (fields[4] - 0.5 * (fields[2] * u + fields[3] * v) - stiff_sum) * (inverse * density)
        return fields[0], fields[1], u, v, p, fields[5]

    def advance_rims(recv, stage):
        dt = dt_ref[0:1, :]
        for side in range(2):
            old = [recv[stage - 1, side, 3 * i : 3 * i + 3] for i in range(6)]
            change = [recv[stage, side, 3 * i : 3 * i + 3] for i in range(6)]
            q_one, q_two, u, v, p, a = old
            density = q_one + q_two
            gamma_sum, stiff_sum = mixture(a)
            energy = gamma_sum * p + stiff_sum + 0.5 * density * (u * u + v * v)
            before = (q_one, q_two, density * u, density * v, energy, a)
            for i, value in enumerate(primitives([b + dt * c for b, c in zip(before, change)])):
                recv[stage, side, 3 * i : 3 * i + 3] = value

    dt_ref[...] = jnp.zeros_like(dt_ref)
    send_axial_rims(0)
    turn_cells(axial_cells, radial_cells)
    send_radial_rims(0)

    def stage_body(stage, carry):
        step = lax.div(stage, 3)
        section = stage - 3 * step
        halos = halo_copies(stage)

        wrapped(axial_cells)
        wrapped(radial_cells)

        early = jnp.logical_and(section == 1, step > 0)

        @pl.when(early)
        def _():
            for copy in halos:
                copy.wait_recv()
            advance_rims(recv_axial, stage)
            advance_rims(recv_radial, stage)
            rim_ghosts(axial_cells, recv_axial, stage, 0, block_first, block_last)
            rim_ghosts(radial_cells, recv_radial, stage, 1, wall, outer)

        radial_sweep()
        axial_ends()

        @pl.when(jnp.logical_not(early))
        def _():
            axial_middle()
            steps_ref[step] = jnp.max(dt_ref[...])
            own_strip(axial_cells, 0)
            own_strip(radial_cells, 1)
            for copy in halo_copies(stage):
                copy.wait_recv()

            @pl.when(section == 1)
            def _():
                advance_rims(recv_axial, stage)
                advance_rims(recv_radial, stage)

            rim_strip(recv_axial, stage, 0, block_first, block_last)
            rim_strip(recv_radial, stage, 1, wall, outer)
            strip_rates()

        @pl.when(jnp.logical_and(section == 0, step > 0))
        def _():
            second_phase(step)

        def turn_back(r, carry):
            for k in range(TURNS):
                i = r * TURNS + k
                block = radial_rate[i, 1 : 1 + TILES].reshape(LANES, LANES)
                turned[i] = block.T.reshape(TILES, ROWS, LANES)
            return carry

        lax.fori_loop(0, 6 // TURNS, turn_back, 0)

        for copy in halos:
            copy.wait_send()

        @pl.when(section == 0)
        def _():
            def rates(t, carry):
                for i, value in enumerate(whole_rate(t, *(axial_cells[i, GHOST + t] for i in range(6)), fields[4, t])):
                    total[0, i, GHOST + t] = value
                return carry

            lax.fori_loop(0, TILES, rates, 0)
            send_axial_rims(stage + 1, total.at[0])
            turn_cells(total.at[0], total.at[1])
            send_radial_rims(stage + 1, total.at[1])
            whole_phase(step, True).wait_recv()
            top = jnp.maximum(max_second[step], jnp.max(got_second[step], axis=0))
            dt = CFL_NUMBER / jnp.broadcast_to(jnp.max(top, axis=1, keepdims=True), (ROWS, LANES))
            dt_ref[...] = dt

        third = jnp.float32(1.0 / 3.0)
        keep = jnp.where(section == 0, 0.0, jnp.where(section == 1, 0.75, third))
        take = jnp.where(section == 0, 1.0, jnp.where(section == 1, 0.25, jnp.float32(2.0 / 3.0)))
        closing = section == 2
        dt = dt_ref[...]

        def update(tiles, most):
            for t in tiles:
                old = [fields[i, t] for i in range(6)]
                change = whole_rate(t, *(axial_cells[i, GHOST + t] for i in range(6)), old[4])
                new = []
                for i in range(6):
                    start = base[i, t]
                    value = keep * start + take * (old[i] + dt * change[i])
                    fields[i, t] = value
                    base[i, t] = jnp.where(closing, value, start)
                    new.append(value)
                q_one, q_two, u, v, p, a = primitives(new)
                for i, value in enumerate((q_one, q_two, u, v, p, a)):
                    axial_cells[i, GHOST + t] = value
                density = q_one + q_two
                gamma_sum, stiff_sum = mixture(a)
                speed = jnp.abs(u) + jnp.abs(v) + celerity_of(density, p, gamma_sum, stiff_sum)
                most = jnp.maximum(most, speed)
            return most

        most = lax.fori_loop(
            0,
            GHOST // RIMS,
            lambda r, m: update([base_tile + r * RIMS + k for k in range(RIMS) for base_tile in (0, TILES - GHOST)], m),
            jnp.zeros((ROWS, LANES), jnp.float32),
        )

        @pl.when(jnp.logical_and(section > 0, stage < STAGES - 1))
        def _():
            send_axial_rims(stage + 1)

        @pl.when(early)
        def _():
            axial_middle()

        most = lax.fori_loop(
            0,
            (TILES - 2 * GHOST) // UPDATES,
            lambda r, m: update([GHOST + r * UPDATES + k for k in range(UPDATES)], m),
            most,
        )

        @pl.when(section == 1)
        def _():
            whole_phase(step, True).wait_send()
            whole_phase(step, False).wait_send()

        @pl.when(jnp.logical_and(closing, step < STEPS - 1))
        def _():
            max_first[step + 1] = jnp.max(most, axis=0, keepdims=True)
            for copy in first_copies(step + 1):
                copy.start()

        @pl.when(stage < STAGES - 1)
        def _():
            turn_cells(axial_cells, radial_cells)

        @pl.when(jnp.logical_and(section > 0, stage < STAGES - 1))
        def _():
            send_radial_rims(stage + 1)

        return carry

    lax.fori_loop(0, STAGES, stage_body, 0)


def finish(ax_size, fields, steps, out_ref, steps_ref):
    outside = lax.axis_index("ax") == ax_size - 1
    lane = lax.broadcasted_iota(jnp.int32, (ROWS, LANES), 1)
    from_lanes = (lane % TILES) * ROWS + lane // TILES
    for i in range(STEPS):
        steps_ref[i] = steps[i]

    def one(r, carry):
        for k in range(FINISHED):
            t = r * FINISHED + k
            for i, value in enumerate(ambient_cell()):
                moved = jnp.take_along_axis(fields[i, t], from_lanes, axis=1)
                out_ref[i, pl.ds(t, ROWS, stride=TILES), :] = jnp.where(outside, jnp.float32(value), moved)
        return carry

    lax.fori_loop(0, TILES // FINISHED, one, 0)


def solution(mesh):
    ax_size, rad_size = mesh.shape["ax"], mesh.shape["rad"]
    sizes = (ax_size // (2 * X_CHIPS), X_CHIPS, 2, rad_size)
    first = sizes[0] * sizes[2] - 1
    second = sizes[1] * sizes[3] - 1

    def shards(labels, jitter):
        block = labels.shape
        f32 = jnp.float32
        tile = (TILES, ROWS, LANES)
        dma = pltpu.SemaphoreType.DMA
        labels, jitter = (pltpu.with_memory_space_constraint(a, pltpu.HBM) for a in (labels, jitter))
        fields, steps = pl.pallas_call(
            functools.partial(kernel, sizes),
            out_shape=(jax.ShapeDtypeStruct((6, *tile), f32), jax.ShapeDtypeStruct((STEPS,), f32)),
            in_specs=[pl.BlockSpec(memory_space=pltpu.HBM)] * 2,
            out_specs=(pl.BlockSpec(memory_space=pltpu.VMEM), pl.BlockSpec(memory_space=pltpu.SMEM)),
            scratch_shapes=[
                pltpu.VMEM(block, jnp.int32),
                pltpu.VMEM(block, f32),
                pltpu.VMEM(block, jnp.int32),
                pltpu.VMEM(block, f32),
                pltpu.VMEM((6, TILES + 2 * GHOST, ROWS, LANES), f32),
                pltpu.VMEM((6, TILES + 2 * GHOST, ROWS, LANES), f32),
                pltpu.VMEM((6, *tile), f32),
                pltpu.VMEM((2, 6, TILES + 3, ROWS, LANES), f32),
                pltpu.VMEM((2, 6, TILES + 3, ROWS, LANES), f32),
                pltpu.VMEM((6, TILES + 2, ROWS, LANES), f32),
                pltpu.VMEM((6, TILES + 2, ROWS, LANES), f32),
                pltpu.VMEM((6, *tile), f32),
                pltpu.VMEM((2, 6, TILES + 2 * GHOST, ROWS, LANES), f32),
                pltpu.VMEM((6, 2, 24, LANES), f32),
                pltpu.VMEM((6, 2, ROWS, LANES), f32),
                pltpu.VMEM((ROWS, LANES), f32),
                pltpu.VMEM((2, 18, 1, LANES), f32),
                pltpu.VMEM((2, 18, 1, LANES), f32),
                pltpu.VMEM((STAGES, 2, 18, 1, LANES), f32),
                pltpu.VMEM((STAGES, 2, 18, 1, LANES), f32),
                pltpu.VMEM((STEPS, 1, LANES), f32),
                pltpu.VMEM((STEPS, 1, LANES), f32),
                pltpu.VMEM((STEPS, first, 1, LANES), f32),
                pltpu.VMEM((STEPS, second, 1, LANES), f32),
                dma((2,)),
                dma((2,)),
                dma((2,)),
                dma((2, 4)),
                dma((2, 4)),
                dma((STEPS,)),
                dma((STEPS,)),
                dma((STEPS,)),
                dma((STEPS,)),
            ],
            compiler_params=pltpu.CompilerParams(
                collective_id=0, has_side_effects=True, vmem_limit_bytes=VMEM_BYTES
            ),
        )(labels, jitter)
        return pl.pallas_call(
            functools.partial(finish, ax_size),
            out_shape=(jax.ShapeDtypeStruct((6, *block), f32), jax.ShapeDtypeStruct((STEPS,), f32)),
            in_specs=[pl.BlockSpec(memory_space=pltpu.VMEM), pl.BlockSpec(memory_space=pltpu.SMEM)],
            out_specs=(pl.BlockSpec(memory_space=pltpu.VMEM), pl.BlockSpec(memory_space=pltpu.SMEM)),
            compiler_params=pltpu.CompilerParams(vmem_limit_bytes=VMEM_BYTES),
        )(fields, steps)

    return jax.shard_map(
        shards, mesh=mesh, in_specs=(P("ax", "rad"),) * 2, out_specs=(P(None, "ax", "rad"), P()), check_vma=False
    )
```
